256 devices in a mesh: seq: 16 (over y_lo, z), chan: 16 (over y_hi, x, core).
Axes of the slice: x: 4, y: 4 (y_hi: 2, y_lo: 2; y = y_hi * 2 + y_lo), z: 8, core: 2. Of those that a mesh axis runs over, the one named last changes fastest.
Arguments:
- tokens: bfloat16 [8192, 8192], P('seq', 'chan'), may hold values from -6 to 6
- norm_gain: float32 [8192], replicated, may hold values from 0.1 to 1.9
- w_in: bfloat16 [8192, 3, 4096], P('seq', None, 'chan'), may hold values from -0.0625 to 0.0625
- short_taps: float32 [3, 3, 4096], P(None, None, 'chan'), may hold values from -3.6 to 3.6
- medium_taps: float32 [128, 256], P(None, 'chan'), may hold values from -0.75 to 0.75
- skip_gain: float32 [4096], P('chan'), may hold values from 0.5 to 1.5
- w_out: bfloat16 [4096, 8192], P('chan'), may hold values from -0.09375 to 0.09375
Outputs:
- block_out: bfloat16 [8192, 8192], P('seq', 'chan')
The draws below stay inside these ranges and needn't reach their ends.
All inputs are finite; a program needn't handle non-finite values.
Results may differ from the reference program's by a relative error of at most 0.019.
Values may be sent and summed in bfloat16 or wider, within the bound.
A program may use at most 128 MiB of HBM per device.

```python
import math
import jax
import jax.numpy as jnp
from jax import lax

D = 8192
HC = 4096
TAPS = 128
GROUP = 16
TOKENS = 8192
FILT = 256
N_CHAN = 16


def draw_medium_taps(key, part):
    rate_key, base_key = jax.random.split(key)
    tap_position = jnp.arange(TAPS, dtype=jnp.float32)[:, None]
    decay_rate = jnp.exp(jax.random.uniform(rate_key, (1, FILT), jnp.float32, math.log(1.0 / 512.0), math.log(1.0 / 12.0)))
    values = jnp.clip(jax.random.normal(base_key, (TAPS, FILT), jnp.float32), -6.0, 6.0)
    return 0.12 * values * jnp.exp(-decay_rate * tap_position)


def block_levels(key, shape, pieces, low, high):
    def one(position, parts):
        heights = jax.random.uniform(jax.random.fold_in(jax.random.fold_in(key, 6), position), (parts,), jnp.float32, low / len(pieces), high / len(pieces))
        return jnp.repeat(jnp.exp(heights), shape[position] // parts).reshape((-1,) + (1,) * (len(shape) - position - 1))

    factor_of = one(*pieces[0])
    for cut in pieces[1:]:
        factor_of = factor_of * one(*cut)
    return factor_of


def gaussian(stream_key, dims, width, most, cuts=(), kind=jnp.bfloat16):
    drawn = width * jax.random.normal(stream_key, dims, jnp.float32)
    if cuts:
        drawn = drawn * block_levels(stream_key, dims, cuts, -0.22, 0.18)
    return jnp.clip(drawn, -most, most).astype(kind)


def setup_inputs(seed: int = 0) -> dict:
    key_of = jax.random.split(jax.random.key(seed), 8)
    tokens = gaussian(key_of[0], (TOKENS, D), 1.0, 6.0, ((0, 16), (1, 16)))
    norm_gain = jnp.clip(1.0 + 0.18 * jax.random.normal(key_of[1], (D,), jnp.float32), 0.1, 1.9)
    w_in = gaussian(key_of[2], (D, 3, HC), D ** -0.5, 0.0625, ((0, 16), (2, 16)))
    short_taps = gaussian(key_of[3], (3, 3, HC), 0.6, 3.6, ((2, 16),), jnp.float32)
    medium_taps = draw_medium_taps(jax.random.fold_in(key_of[7], 71), 0)
    skip_gain = jnp.clip(0.5 + 1.0 * jax.random.uniform(key_of[5], (HC,), jnp.float32) ** block_levels(key_of[5], (HC,), ((0, 16),), -0.2, 0.2), 0.5, 1.5)
    w_out = gaussian(key_of[6], (HC, D), HC ** -0.5, 0.09375, ((0, 16),))
    return {"tokens": tokens, "norm_gain": norm_gain, "w_in": w_in, "short_taps": short_taps, "medium_taps": medium_taps, "skip_gain": skip_gain, "w_out": w_out}


EPSILON = 1e-06

def delayed(values, lag_rows):
    padding = jnp.zeros((lag_rows,) + values.shape[1:], values.dtype)
    return jnp.concatenate([padding, values[:values.shape[0] - lag_rows]], 0)

def reference(tokens, norm_gain, w_in, short_taps, medium_taps, skip_gain, w_out):
    widened = tokens.astype(jnp.float32)
    mean_square = lax.optimization_barrier(jnp.mean(widened * widened, axis=1, keepdims=True))
    normed = (widened * lax.rsqrt(mean_square + EPSILON) * norm_gain).astype(jnp.bfloat16)
    projected = jnp.dot(normed, w_in.reshape(D, 3 * HC), preferred_element_type=jnp.float32)
    projected = lax.optimization_barrier(projected.astype(jnp.bfloat16))
    projected = projected.reshape(TOKENS, 3, HC).astype(jnp.float32)
    filtered = short_taps[0] * projected + short_taps[1] * delayed(projected, 1) + short_taps[2] * delayed(projected, 2)
    product = lax.optimization_barrier((filtered[:, 1] * filtered[:, 2]).astype(jnp.bfloat16)).astype(jnp.float32)
    per_channel = jnp.repeat(medium_taps, GROUP, axis=1)
    padded = jnp.concatenate([jnp.zeros((TAPS - 1, HC), jnp.float32), product], 0)

    def add_tap(tap_index, running):
        offset = (TAPS - 1 - tap_index).astype(jnp.int32)
        window = lax.dynamic_slice_in_dim(padded, offset, TOKENS, 0)
        weights = lax.dynamic_index_in_dim(per_channel, tap_index.astype(jnp.int32), 0, keepdims=False)
        return running + weights * window
    mixing = lax.fori_loop(0, TAPS, add_tap, skip_gain * product)
    gating = (filtered[:, 0] * mixing).astype(jnp.bfloat16)
    shard_width = HC // N_CHAN

    def add_shard(running, shard_index):
        start = (shard_index * shard_width).astype(jnp.int32)
        columns = lax.dynamic_slice_in_dim(gating, start, shard_width, 1)
        rows = lax.dynamic_slice_in_dim(w_out, start, shard_width, 0)
        partial_sum = jnp.dot(columns, rows, preferred_element_type=jnp.float32)
        rounded = lax.optimization_barrier(partial_sum.astype(jnp.bfloat16)).astype(jnp.float32)
        return (running + rounded, None)
    summed, _ = lax.scan(add_shard, jnp.zeros((TOKENS, D), jnp.float32), jnp.arange(N_CHAN, dtype=jnp.int32))
    output = widened + summed
    return output.astype(jnp.bfloat16)
```

```python
import functools
import jax
import jax.numpy as jnp
from jax import lax
from jax.experimental import pallas as pl
from jax.experimental.pallas import tpu as pltpu
from jax.sharding import PartitionSpec as P

TAPS = 128
GROUP = 16
EPSILON = 1e-06
MESH = pl.DeviceIdType.MESH
ROWS = 512
WIDE = 512
CH = 256
F32 = jnp.float32
BF16 = jnp.bfloat16


def project_kernel(
    x_hbm, gain_ref, w_hbm, out_ref,
    tok, tg, wb, acc, cs, cr, sq, ss, sr,
    loc, w_send, w_recv, y_send, y_recv, x_send, x_recv, d_send, d_recv, c_send, c_recv, s_send, s_recv,
):
    s = lax.axis_index("seq")
    c = lax.axis_index("chan")
    y_lo, z = s // 8, s % 8
    y_hi, x, core = c // 8, (c // 2) % 4, c % 2
    f_own = x * 2 + core
    x_right, x_left, x_far = (x + 1) % 4, (x + 3) % 4, (x + 2) % 4

    def at(y_hi_=y_hi, x_=x, core_=core, y_lo_=y_lo, z_=z):
        return (y_lo_ * 8 + z_, y_hi_ * 8 + x_ * 2 + core_)

    right, left = at(x_=x_right), at(x_=x_left)
    up, down = at(z_=(z + 1) % 8), at(z_=(z + 7) % 8)
    twin = at(core_=1 - core)
    mate = at(y_lo_=1 - y_lo)
    opposite = at(y_hi_=1 - y_hi)
    diagonal = at(y_hi_=1 - y_hi, y_lo_=1 - y_lo)

    def remote(src, dst, send, recv, device):
        return pltpu.make_async_remote_copy(
            src_ref=src, dst_ref=dst, send_sem=send, recv_sem=recv, device_id=device, device_id_type=MESH
        )

    own_w = [
        pltpu.make_async_copy(w_hbm.at[:, pl.ds(h * 256, 256), :], wb.at[z, h], loc.at[h]) for h in range(2)
    ]
    for cp in own_w:
        cp.start()

    barrier = pltpu.get_barrier_semaphore()
    peers = (right, left, up, down, twin, mate, opposite, diagonal)
    for peer in peers:
        pl.semaphore_signal(barrier, inc=1, device_id=peer, device_id_type=MESH)
    pl.semaphore_wait(barrier, len(peers))

    def w_slot(direction, distance, half, ahead=0):
        source = (z + 8 - distance) % 8 if direction == 0 else (z + distance) % 8
        return wb.at[source, half]

    def recv_place(direction, k):
        if k == 6:
            return 4, direction
        return k // 2 + 1, k % 2

    def send_place(direction, k):
        if k < 2:
            return 0, k
        if k == 6:
            return 3, direction
        return (k - 2) // 2 + 1, (k - 2) % 2

    def w_copy(direction, k):
        slot = w_slot(direction, *send_place(direction, k))
        return remote(slot, slot, w_send.at[direction, k], w_recv.at[direction, k], up if direction == 0 else down)

    def w_wait(direction, k):
        slot = w_slot(direction, *recv_place(direction, k))
        remote(slot, slot, w_send.at[direction, k], w_recv.at[direction, k], up).wait_recv()

    for h in range(2):
        own_w[h].wait()
        for direction in range(2):
            w_copy(direction, h).start()

    is_home = y_hi == y_lo
    def y_copy(d):
        slot = tok.at[y_lo, f_own]
        return remote(x_hbm, slot, y_send.at[d], y_recv.at[y_lo], at(y_lo_=y_hi, y_hi_=d))

    own_x = pltpu.make_async_copy(x_hbm, tok.at[y_lo, f_own], loc.at[2])
    for d in range(2):
        stays = jnp.logical_and(is_home, y_hi == d)

        @pl.when(jnp.logical_not(stays))
        def _():
            y_copy(d).start()

        @pl.when(stays)
        def _():
            own_x.start()

    def step(k):
        for direction in range(2):
            w_wait(direction, k - 2)
            if k < 6:
                w_copy(direction, k).start()

    acc[...] = jnp.zeros_like(acc)
    sq[...] = jnp.zeros_like(sq)

    step(2)

    for u in range(2):
        stays = jnp.logical_and(is_home, y_lo == u)
        slot = tok.at[u, f_own]

        @pl.when(jnp.logical_not(stays))
        def _():
            remote(slot, slot, y_send.at[0], y_recv.at[u], right).wait_recv()

        @pl.when(stays)
        def _():
            pltpu.make_async_copy(x_hbm, slot, loc.at[2]).wait()

    def x_copy(direction, k):
        device = right if direction == 0 else left
        if k < 2:
            u = k if direction == 0 else 1 - k
            slot = tok.at[u, f_own]
        else:
            slot = tok.at[direction, (x_left if direction == 0 else x_right) * 2 + core]
        return remote(slot, slot, x_send.at[direction, k], x_recv.at[direction, k], device)

    def x_place(direction, k):
        near = x_left if direction == 0 else x_right
        if k < 2:
            u = k if direction == 0 else 1 - k
            return u, near
        return direction, x_far

    def x_wait(direction, k):
        u, source = x_place(direction, k)
        slot = tok.at[u, source * 2 + core]
        remote(slot, slot, x_send.at[direction, k], x_recv.at[direction, k], right).wait_recv()

    def d_copy(index, u, source, core_):
        slot = tok.at[u, source * 2 + core_]
        return remote(slot, slot, d_send.at[index], d_recv.at[index], twin)

    places = [(0, x), (1, x)]
    for k in range(3):
        for direction in range(2):
            places.append(x_place(direction, k))

    for k in range(2):
        for direction in range(2):
            x_copy(direction, k).start()
    for index in range(2):
        d_copy(index, *places[index], core).start()

    def scaled(u, f):
        def body(i, carry):
            rows = pl.ds(pl.multiple_of(i * 64, 64), 64)
            raw = tok[u, f, rows, :].astype(F32)
            gain = gain_ref[pl.ds(y_lo * 8 + f, 1), 0, :]
            tg[u, f, rows, :] = (raw * gain).astype(BF16)
            square = raw * raw
            total = square[:, 0:128] + square[:, 128:256] + square[:, 256:384] + square[:, 384:512]
            sq[u, rows, :] += total
            return carry

        lax.fori_loop(0, 8, body, 0)

    def taken(index):
        u, source = places[index]
        scaled(u, source * 2 + core)
        d_copy(index, u, source, 1 - core).wait_recv()
        scaled(u, source * 2 + 1 - core)

    step(3)
    taken(0)
    taken(1)
    step(4)
    for direction in range(2):
        x_wait(direction, 0)
        x_copy(direction, 2).start()
        d_copy(2 + direction, *places[2 + direction], core).start()
    step(5)
    for direction in range(2):
        x_wait(direction, 1)
        d_copy(4 + direction, *places[4 + direction], core).start()
    for index in range(2, 6):
        taken(index)
    for direction in range(2):
        w_wait(direction, 4)
        w_wait_other = None
        if direction == 0:
            w_copy(0, 6).start()
    for direction in range(2):
        w_wait(direction, 5)
        if direction == 1:
            w_copy(1, 6).start()
    for direction in range(2):
        x_wait(direction, 2)
        d_copy(6 + direction, *places[6 + direction], core).start()
    for index in range(6, 8):
        taken(index)

    other = 1 - y_lo

    def row_sums(u):
        column = jnp.sum(sq[u], axis=1, keepdims=True)
        return jnp.transpose(jnp.broadcast_to(column, (ROWS, 128)))[0:8, :]

    ss[...] = row_sums(other)
    s_copy = remote(ss, sr, s_send, s_recv, mate)
    s_copy.start()

    def multiply(u, f, i):
        rows = pl.ds(pl.multiple_of(i * 256, 256), 256)
        lhs0 = tg[u, f, rows, 0:256]
        lhs1 = tg[u, f, rows, 256:512]
        parts = []
        for p in range(3):
            part = jnp.dot(lhs0, wb[f, 0, p], preferred_element_type=F32)
            part += jnp.dot(lhs1, wb[f, 1, p], preferred_element_type=F32)
            parts.append(part)
        return rows, parts

    def add_chunk(f):
        def body(i, carry):
            u, i = i // 2, i % 2
            rows, parts = multiply(u, f, i)
            for p in range(3):
                acc[u, p, rows, :] += parts[p]
            return carry

        lax.fori_loop(0, 4, body, 0)

    def chunk_loop(j, carry):
        add_chunk((z + 5 + j) % 8)
        return carry

    lax.fori_loop(0, 7, chunk_loop, 0)
    for direction in range(2):
        w_wait(direction, 6)
    f_last = (z + 4) % 8

    def c_copy(i):
        rows = pl.ds(i * 256, 256)
        return remote(cs.at[:, rows, :], cr.at[:, rows, :], c_send.at[i], c_recv.at[i], mate)

    for i in (1, 0):
        rows, parts = multiply(other, f_last, i)
        for p in range(3):
            cs[p, rows, :] = (acc[other, p, rows, :] + parts[p]).astype(BF16)
        c_copy(i).start()

    s_copy.wait()
    total = row_sums(y_lo) + sr[...]
    factor = lax.rsqrt(total * (1.0 / 8192.0) + EPSILON)
    factor = jnp.transpose(jnp.broadcast_to(factor[0:1, :], (128, ROWS)))
    sq[0] = factor
    for i in (1, 0):
        rows, parts = multiply(y_lo, f_last, i)
        for p in range(3):
            acc[y_lo, p, rows, :] += parts[p]
    for i in (1, 0):
        rows = pl.ds(i * 256, 256)
        c_copy(i).wait_recv()
        factor = sq[0, rows, :]
        factor = jnp.concatenate([factor, factor], axis=1)
        for p in range(3):
            value = acc[y_lo, p, rows, :] + cr[p, rows, :].astype(F32)
            out_ref[p, rows, :] = (value * factor).astype(BF16)

    for direction in range(2):
        for k in range(7):
            w_copy(direction, k).wait_send()
        for k in range(3):
            x_copy(direction, k).wait_send()
    for d in range(2):
        @pl.when(jnp.logical_not(jnp.logical_and(is_home, y_hi == d)))
        def _():
            y_copy(d).wait_send()
    for index in range(8):
        d_copy(index, *places[index], core).wait_send()
    for i in range(2):
        c_copy(i).wait_send()


def project(tokens, gain, w_planes):
    dma = pltpu.SemaphoreType.DMA
    return pl.pallas_call(
        project_kernel,
        out_shape=jax.ShapeDtypeStruct((3, ROWS, CH), BF16),
        in_specs=[
            pl.BlockSpec(memory_space=pl.ANY),
            pl.BlockSpec(memory_space=pltpu.VMEM),
            pl.BlockSpec(memory_space=pl.ANY),
        ],
        out_specs=pl.BlockSpec(memory_space=pltpu.VMEM),
        scratch_shapes=[
            pltpu.VMEM((2, 8, ROWS, WIDE), BF16),
            pltpu.VMEM((2, 8, ROWS, WIDE), BF16),
            pltpu.VMEM((8, 2, 3, 256, CH), BF16),
            pltpu.VMEM((2, 3, ROWS, CH), F32),
            pltpu.VMEM((3, ROWS, CH), BF16),
            pltpu.VMEM((3, ROWS, CH), BF16),
            pltpu.VMEM((2, ROWS, 128), F32),
            pltpu.VMEM((8, ROWS), F32),
            pltpu.VMEM((8, ROWS), F32),
            dma((3,)),
            dma((2, 7)), dma((2, 7)),
            dma((2,)), dma((2,)),
            dma((2, 3)), dma((2, 3)),
            dma((8,)), dma((8,)),
            dma((2,)), dma((2,)),
            dma, dma,
        ],
        compiler_params=pltpu.CompilerParams(
            collective_id=0, has_side_effects=True, vmem_limit_bytes=56 * 1024 * 1024
        ),
        name="project",
    )(tokens, gain, w_planes)


def passed_along(value, axis, steps):
    count = lax.axis_size(axis)
    first, last = (max(0, -steps), min(count, count - steps))
    return lax.ppermute(value, axis, [(source, source + steps) for source in range(first, last)])


def short_filter(extended, taps):
    return taps[0] * extended[2:] + taps[1] * extended[1:-1] + taps[2] * extended[:-2]


def per_device(tokens, norm_gain, w_in, short_taps, medium_taps, skip_gain, w_out):
    row_count = tokens.shape[0]
    channels = w_in.shape[2]
    planes = project(tokens, norm_gain.reshape(16, 1, WIDE), jnp.transpose(w_in, (1, 0, 2)))
    projected = jnp.transpose(planes, (1, 0, 2))
    edge_rows = passed_along(projected[row_count - 2 :], "seq", 1)
    extended = lax.optimization_barrier(jnp.concatenate([edge_rows, projected], 0)).astype(
        jnp.float32
    )
    filtered = short_filter(extended, short_taps)
    queries = filtered[:, 0]
    product = (filtered[:, 1] * filtered[:, 2]).astype(jnp.bfloat16)
    product_rows = passed_along(product[row_count - (TAPS - 1) :], "seq", 1)
    reached = jnp.concatenate([product_rows, product], 0)
    floats = lax.optimization_barrier(reached).astype(jnp.float32)
    padded = jnp.concatenate([jnp.zeros((1, channels), jnp.float32), floats], 0)
    block_count = row_count // TAPS
    blocks = padded.reshape(block_count + 1, TAPS, channels)
    windows = jnp.concatenate([blocks[:-1], blocks[1:]], 1)
    cube_shape = (TAPS, TAPS, 2 * TAPS)
    lagged = (
        lax.broadcasted_iota(jnp.int32, cube_shape, 1)
        + TAPS
        - lax.broadcasted_iota(jnp.int32, cube_shape, 2)
    )
    onehot = (lagged == lax.broadcasted_iota(jnp.int32, cube_shape, 0)).astype(jnp.float32)
    toeplitz = jnp.einsum("jg,jis->gis", medium_taps, onehot, precision=lax.Precision.HIGHEST)
    filters = medium_taps.shape[1]
    grouped = windows.reshape(block_count, 2 * TAPS, filters, GROUP)
    convolved = jnp.einsum("gis,bsgc->bigc", toeplitz, grouped, precision=lax.Precision.HIGHEST)
    mixing = skip_gain * floats[TAPS - 1 :] + convolved.reshape(row_count, channels)
    gating = (queries * mixing).astype(jnp.bfloat16)
    partial_out = jnp.dot(gating, w_out, preferred_element_type=jnp.float32)
    rounded_out = lax.optimization_barrier(partial_out.astype(jnp.bfloat16)).astype(jnp.float32)
    projected_out = lax.psum_scatter(
        rounded_out.astype(jnp.bfloat16), "chan", scatter_dimension=1, tiled=True
    ).astype(jnp.float32)
    return (tokens.astype(jnp.float32) + projected_out).astype(jnp.bfloat16)


def solution(mesh):
    in_specs = (
        P("seq", "chan"),
        P(),
        P("seq", None, "chan"),
        P(None, None, "chan"),
        P(None, "chan"),
        P("chan"),
        P("chan", None),
    )
    out_specs = P("seq", "chan")
    return jax.shard_map(
        per_device, mesh=mesh, in_specs=in_specs, out_specs=out_specs, check_vma=False
    )
```

```python
import jax
import jax.numpy as jnp
from jax import lax
from jax.experimental import pallas as pl
from jax.experimental.pallas import tpu as pltpu
from jax.sharding import PartitionSpec as P

TAPS = 128
GROUP = 16
EPSILON = 1e-06
MESH = pl.DeviceIdType.MESH
ROWS = 512
WIDE = 512
CH = 256
F32 = jnp.float32
BF16 = jnp.bfloat16


def block_kernel(
    x_hbm, gain_ref, w_hbm, short_ref, taps_ref, skip_ref, wo_hbm, out_ref,
    tok, tg, wb, acc, cs, cr, sq, ss, sr, wo, toep, pj, pe, gate, sb, rb, yb, yr, xres,
    loc, w_send, w_recv, y_send, y_recv, x_send, x_recv, d_send, d_recv, c_send, c_recv, s_send, s_recv,
    o_loc, o_send, o_recv, h_send, h_recv, g_send, g_recv, r_send, r_recv, v_send, v_recv,
):
    s = lax.axis_index("seq")
    c = lax.axis_index("chan")
    y_lo, z = s // 8, s % 8
    y_hi, x, core = c // 8, (c // 2) % 4, c % 2
    f_own = x * 2 + core
    x_right, x_left, x_far = (x + 1) % 4, (x + 3) % 4, (x + 2) % 4

    def at(y_hi_=y_hi, x_=x, core_=core, y_lo_=y_lo, z_=z):
        return (y_lo_ * 8 + z_, y_hi_ * 8 + x_ * 2 + core_)

    right, left = at(x_=x_right), at(x_=x_left)
    up, down = at(z_=(z + 1) % 8), at(z_=(z + 7) % 8)
    twin = at(core_=1 - core)
    mate = at(y_lo_=1 - y_lo)
    opposite = at(y_hi_=1 - y_hi)
    diagonal = at(y_hi_=1 - y_hi, y_lo_=1 - y_lo)
    after, before = ((s + 1) % 16, c), ((s + 15) % 16, c)

    def remote(src, dst, send, recv, device):
        return pltpu.make_async_remote_copy(
            src_ref=src, dst_ref=dst, send_sem=send, recv_sem=recv, device_id=device, device_id_type=MESH
        )

    own_w = [
        pltpu.make_async_copy(w_hbm.at[:, pl.ds(h * 256, 256), :], wb.at[z, h], loc.at[h]) for h in range(2)
    ]
    for cp in own_w:
        cp.start()

    barrier = pltpu.get_barrier_semaphore()
    peers = (right, left, up, down, twin, mate, opposite, diagonal, after, before)
    for peer in peers:
        pl.semaphore_signal(barrier, inc=1, device_id=peer, device_id_type=MESH)
    pl.semaphore_wait(barrier, len(peers))

    def w_slot(direction, distance, half, ahead=0):
        source = (z + 8 - distance) % 8 if direction == 0 else (z + distance) % 8
        return wb.at[source, half]

    def recv_place(direction, k):
        if k == 6:
            return 4, direction
        return k // 2 + 1, k % 2

    def send_place(direction, k):
        if k < 2:
            return 0, k
        if k == 6:
            return 3, direction
        return (k - 2) // 2 + 1, (k - 2) % 2

    def w_copy(direction, k):
        slot = w_slot(direction, *send_place(direction, k))
        return remote(slot, slot, w_send.at[direction, k], w_recv.at[direction, k], up if direction == 0 else down)

    def w_wait(direction, k):
        slot = w_slot(direction, *recv_place(direction, k))
        remote(slot, slot, w_send.at[direction, k], w_recv.at[direction, k], up).wait_recv()

    for h in range(2):
        own_w[h].wait()
        for direction in range(2):
            w_copy(direction, h).start()

    is_home = y_hi == y_lo
    def y_copy(d):
        slot = tok.at[y_lo, f_own]
        return remote(x_hbm, slot, y_send.at[d], y_recv.at[y_lo], at(y_lo_=y_hi, y_hi_=d))

    own_x = pltpu.make_async_copy(x_hbm, tok.at[y_lo, f_own], loc.at[2])
    for d in range(2):
        stays = jnp.logical_and(is_home, y_hi == d)

        @pl.when(jnp.logical_not(stays))
        def _():
            y_copy(d).start()

        @pl.when(stays)
        def _():
            own_x.start()

    def step(k):
        for direction in range(2):
            w_wait(direction, k - 2)
            if k < 6:
                w_copy(direction, k).start()

    def columns(d, core_):
        return wo_hbm.at[:, pl.ds(pl.multiple_of((d * 2 + core_) * WIDE, WIDE), WIDE)]

    def o_keep(d):
        return pltpu.make_async_copy(columns(d, core), wo.at[core, d], o_loc.at[d])

    def o_copy(d):
        return remote(columns(d, 1 - core), wo.at[core, d], o_send.at[d], o_recv.at[d], twin)

    for d in range(8):
        o_copy(d).start()
        o_keep(d).start()
    keep_x = pltpu.make_async_copy(x_hbm, xres, loc.at[3])
    keep_x.start()

    acc[...] = jnp.zeros_like(acc)
    sq[...] = jnp.zeros_like(sq)

    spread = (
        lax.broadcasted_iota(jnp.int32, (TAPS, 2 * TAPS), 0) + lax.broadcasted_iota(jnp.int32, (TAPS, 2 * TAPS), 1)
        == TAPS
    ).astype(F32)
    first = jnp.dot(taps_ref[...], spread, precision=lax.Precision.HIGHEST, preferred_element_type=F32)
    for g in range(16):
        row = jnp.broadcast_to(first[g : g + 1, :], (TAPS, 2 * TAPS))
        matrix = pltpu.roll(row, 0, 1, stride=1, stride_axis=0)
        high = matrix.astype(BF16)
        toep[0, g] = high
        toep[1, g] = (matrix - high.astype(F32)).astype(BF16)

    step(2)

    for u in range(2):
        stays = jnp.logical_and(is_home, y_lo == u)
        slot = tok.at[u, f_own]

        @pl.when(jnp.logical_not(stays))
        def _():
            remote(slot, slot, y_send.at[0], y_recv.at[u], right).wait_recv()

        @pl.when(stays)
        def _():
            pltpu.make_async_copy(x_hbm, slot, loc.at[2]).wait()

    def x_copy(direction, k):
        device = right if direction == 0 else left
        if k < 2:
            u = k if direction == 0 else 1 - k
            slot = tok.at[u, f_own]
        else:
            slot = tok.at[direction, (x_left if direction == 0 else x_right) * 2 + core]
        return remote(slot, slot, x_send.at[direction, k], x_recv.at[direction, k], device)

    def x_place(direction, k):
        near = x_left if direction == 0 else x_right
        if k < 2:
            u = k if direction == 0 else 1 - k
            return u, near
        return direction, x_far

    def x_wait(direction, k):
        u, source = x_place(direction, k)
        slot = tok.at[u, source * 2 + core]
        remote(slot, slot, x_send.at[direction, k], x_recv.at[direction, k], right).wait_recv()

    def d_copy(index, u, source, core_):
        slot = tok.at[u, source * 2 + core_]
        return remote(slot, slot, d_send.at[index], d_recv.at[index], twin)

    places = [(0, x), (1, x)]
    for k in range(3):
        for direction in range(2):
            places.append(x_place(direction, k))

    for k in range(2):
        for direction in range(2):
            x_copy(direction, k).start()
    for index in range(2):
        d_copy(index, *places[index], core).start()

    def scaled(u, f):
        def body(i, carry):
            rows = pl.ds(pl.multiple_of(i * 64, 64), 64)
            raw = tok[u, f, rows, :].astype(F32)
            gain = gain_ref[pl.ds(y_lo * 8 + f, 1), 0, :]
            tg[u, f, rows, :] = (raw * gain).astype(BF16)
            square = raw * raw
            total = square[:, 0:128] + square[:, 128:256] + square[:, 256:384] + square[:, 384:512]
            sq[u, rows, :] += total
            return carry

        lax.fori_loop(0, 8, body, 0)

    def taken(index):
        u, source = places[index]
        scaled(u, source * 2 + core)
        d_copy(index, u, source, 1 - core).wait_recv()
        scaled(u, source * 2 + 1 - core)

    step(3)
    taken(0)
    taken(1)
    step(4)
    for direction in range(2):
        x_wait(direction, 0)
        x_copy(direction, 2).start()
        d_copy(2 + direction, *places[2 + direction], core).start()
    step(5)
    for direction in range(2):
        x_wait(direction, 1)
        d_copy(4 + direction, *places[4 + direction], core).start()
    for index in range(2, 6):
        taken(index)
    for direction in range(2):
        w_wait(direction, 4)
        w_wait_other = None
        if direction == 0:
            w_copy(0, 6).start()
    for direction in range(2):
        w_wait(direction, 5)
        if direction == 1:
            w_copy(1, 6).start()
    for direction in range(2):
        x_wait(direction, 2)
        d_copy(6 + direction, *places[6 + direction], core).start()
    for index in range(6, 8):
        taken(index)

    other = 1 - y_lo

    def row_sums(u):
        column = jnp.sum(sq[u], axis=1, keepdims=True)
        return jnp.transpose(jnp.broadcast_to(column, (ROWS, 128)))[0:8, :]

    ss[...] = row_sums(other)
    s_copy = remote(ss, sr, s_send, s_recv, mate)
    s_copy.start()

    def multiply(u, f, i):
        rows = pl.ds(pl.multiple_of(i * 256, 256), 256)
        lhs0 = tg[u, f, rows, 0:256]
        lhs1 = tg[u, f, rows, 256:512]
        parts = []
        for p in range(3):
            part = jnp.dot(lhs0, wb[f, 0, p], preferred_element_type=F32)
            part += jnp.dot(lhs1, wb[f, 1, p], preferred_element_type=F32)
            parts.append(part)
        return rows, parts

    def add_chunk(f):
        def body(i, carry):
            u, i = i // 2, i % 2
            rows, parts = multiply(u, f, i)
            for p in range(3):
                acc[u, p, rows, :] += parts[p]
            return carry

        lax.fori_loop(0, 4, body, 0)

    def chunk_loop(j, carry):
        add_chunk((z + 5 + j) % 8)
        return carry

    lax.fori_loop(0, 7, chunk_loop, 0)
    for direction in range(2):
        w_wait(direction, 6)
    f_last = (z + 4) % 8

    def c_copy(i):
        rows = pl.ds(i * 256, 256)
        return remote(cs.at[:, rows, :], cr.at[:, rows, :], c_send.at[i], c_recv.at[i], mate)

    for i in (1, 0):
        rows, parts = multiply(other, f_last, i)
        for p in range(3):
            cs[p, rows, :] = (acc[other, p, rows, :] + parts[p]).astype(BF16)
        c_copy(i).start()

    s_copy.wait()
    total = row_sums(y_lo) + sr[...]
    factor = lax.rsqrt(total * (1.0 / 8192.0) + EPSILON)
    factor = jnp.transpose(jnp.broadcast_to(factor[0:1, :], (128, ROWS)))
    sq[0] = factor
    for i in (1, 0):
        rows, parts = multiply(y_lo, f_last, i)
        for p in range(3):
            acc[y_lo, p, rows, :] += parts[p]
    def finish(i):
        rows = pl.ds(i * 256, 256)
        c_copy(i).wait_recv()
        factor = sq[0, rows, :]
        factor = jnp.concatenate([factor, factor], axis=1)
        for p in range(3):
            value = acc[y_lo, p, rows, :] + cr[p, rows, :].astype(F32)
            pj[p, pl.ds(16 + i * 256, 256), :] = (value * factor).astype(BF16)

    def filtered(p, r):
        extended = pj[p, pl.ds(r * 128, 144), :].astype(F32)
        taps = [short_ref[k, pl.ds(p, 1), :] for k in range(3)]
        return taps[0] * extended[16:144] + taps[1] * extended[15:143] + taps[2] * extended[14:142]

    def make_product(r):
        pe[pl.ds(128 + r * 128, 128), :] = (filtered(1, r) * filtered(2, r)).astype(BF16)

    halo_out = [
        remote(pe.at[pl.ds(512, 128), :], pe.at[pl.ds(0, 128), :], h_send.at[0], h_recv.at[0], after),
        remote(pj.at[:, pl.ds(512, 16), :], pj.at[:, pl.ds(0, 16), :], h_send.at[1], h_recv.at[1], after),
    ]

    group_of_lane = lax.broadcasted_iota(jnp.int32, (128, CH), 1) // GROUP

    def g_copy(r):
        place = gate.at[core, pl.ds(r * 128, 128), :]
        return remote(place, place, g_send.at[r], g_recv.at[r], twin)

    def make_gating(r):
        window = pe[pl.ds(r * 128, 256), :]

        def body(g, mixed):
            part = jnp.dot(toep[0, g], window, preferred_element_type=F32)
            part += jnp.dot(toep[1, g], window, preferred_element_type=F32)
            return jnp.where(group_of_lane == g, part, mixed)

        mixed = lax.fori_loop(0, 16, body, jnp.zeros((128, CH), F32), unroll=4)
        product = pe[pl.ds(128 + r * 128, 128), :].astype(F32)
        mixing = skip_ref[...] * product + mixed
        gate[core, pl.ds(r * 128, 128), :] = (filtered(0, r) * mixing).astype(BF16)
        g_copy(r).start()

    def block(r, x_, y_hi_):
        d = y_hi_ * 4 + x_
        rows = pl.ds(r * 128, 128)
        part = jnp.dot(gate[0, rows, :], wo[0, d], preferred_element_type=F32)
        return part + jnp.dot(gate[1, rows, :], wo[1, d], preferred_element_type=F32)

    def r_copy(r, direction, k):
        return remote(
            sb.at[r, direction, k], rb.at[r, direction, k], r_send.at[r, direction, k], r_recv.at[r, direction, k],
            right if direction == 0 else left,
        )

    def v_copy(r):
        return remote(yb.at[r], yr.at[r], v_send.at[r], v_recv.at[r], opposite)

    nears = (x_right, x_left)

    def send_first(r):
        twin_place = gate.at[1 - core, pl.ds(r * 128, 128), :]
        remote(twin_place, twin_place, g_send.at[r], g_recv.at[r], twin).wait_recv()
        for direction in range(2):
            sb[r, direction, 0] = block(r, x_far, direction).astype(BF16)
            r_copy(r, direction, 0).start()
        for direction in range(2):
            sb[r, direction, 1] = block(r, nears[direction], 1 - direction).astype(BF16)
            r_copy(r, direction, 1).start()

    def send_joined(r):
        for direction in range(2):
            mine = block(r, nears[direction], direction)
            r_copy(r, direction, 0).wait_recv()
            sb[r, direction, 2] = (mine + rb[r, direction, 0].astype(F32)).astype(BF16)
            r_copy(r, direction, 2).start()

    def summed(r, y_hi_):
        mine = block(r, x, y_hi_)
        alone, joined = rb[r, 1 - y_hi_, 1], rb[r, y_hi_, 2]
        return mine + alone.astype(F32) + joined.astype(F32)

    def send_across(r):
        for direction in range(2):
            r_copy(r, direction, 1).wait_recv()
            r_copy(r, direction, 2).wait_recv()
        yb[r] = summed(r, 1 - y_hi).astype(BF16)
        v_copy(r).start()

    def write(r):
        rows = pl.ds(r * 128, 128)
        mine = summed(r, y_hi) + xres[rows, :].astype(F32)
        v_copy(r).wait_recv()
        out_ref[rows, :] = (mine + yr[r].astype(F32)).astype(BF16)

    finish(1)
    make_product(3)

    @pl.when(s < 15)
    def _():
        for cp in halo_out:
            cp.start()

    @pl.when(s == 0)
    def _():
        pe[pl.ds(0, 128), :] = jnp.zeros((128, CH), BF16)
        pj[:, pl.ds(0, 16), :] = jnp.zeros((3, 16, CH), BF16)

    finish(0)
    make_product(2)
    for d in range(8):
        o_keep(d).wait()
        remote(wo.at[1 - core, d], wo.at[1 - core, d], o_send.at[d], o_recv.at[d], twin).wait_recv()
    keep_x.wait()
    make_gating(3)
    make_product(1)
    send_first(3)
    make_gating(2)
    send_first(2)

    @pl.when(s > 0)
    def _():
        for cp in halo_out:
            cp.wait_recv()

    make_product(0)
    make_gating(1)
    send_joined(3)
    send_first(1)
    make_gating(0)
    send_joined(2)
    send_first(0)
    send_across(3)
    send_joined(1)
    send_across(2)
    write(3)
    send_joined(0)
    send_across(1)
    write(2)
    send_across(0)
    write(1)
    write(0)

    for direction in range(2):
        for k in range(7):
            w_copy(direction, k).wait_send()
        for k in range(3):
            x_copy(direction, k).wait_send()
    for d in range(2):
        @pl.when(jnp.logical_not(jnp.logical_and(is_home, y_hi == d)))
        def _():
            y_copy(d).wait_send()
    for index in range(8):
        d_copy(index, *places[index], core).wait_send()
    for i in range(2):
        c_copy(i).wait_send()
    for d in range(8):
        o_copy(d).wait_send()
    for r in range(4):
        g_copy(r).wait_send()
        v_copy(r).wait_send()
        for direction in range(2):
            for k in range(3):
                r_copy(r, direction, k).wait_send()

    @pl.when(s < 15)
    def _():
        for cp in halo_out:
            cp.wait_send()


def block_call(tokens, gain, w_planes, short_taps, taps, skip, w_out):
    dma = pltpu.SemaphoreType.DMA
    vmem = pl.BlockSpec(memory_space=pltpu.VMEM)
    far = pl.BlockSpec(memory_space=pl.ANY)
    return pl.pallas_call(
        block_kernel,
        out_shape=jax.ShapeDtypeStruct((ROWS, WIDE), BF16),
        in_specs=[far, vmem, far, vmem, vmem, vmem, far],
        out_specs=vmem,
        scratch_shapes=[
            pltpu.VMEM((2, 8, ROWS, WIDE), BF16),
            pltpu.VMEM((2, 8, ROWS, WIDE), BF16),
            pltpu.VMEM((8, 2, 3, 256, CH), BF16),
            pltpu.VMEM((2, 3, ROWS, CH), F32),
            pltpu.VMEM((3, ROWS, CH), BF16),
            pltpu.VMEM((3, ROWS, CH), BF16),
            pltpu.VMEM((2, ROWS, 128), F32),
            pltpu.VMEM((8, ROWS), F32),
            pltpu.VMEM((8, ROWS), F32),
            pltpu.VMEM((2, 8, CH, WIDE), BF16),
            pltpu.VMEM((2, 16, TAPS, 2 * TAPS), BF16),
            pltpu.VMEM((3, 16 + ROWS, CH), BF16),
            pltpu.VMEM((128 + ROWS, CH), BF16),
            pltpu.VMEM((2, ROWS, CH), BF16),
            pltpu.VMEM((4, 2, 3, 128, WIDE), BF16),
            pltpu.VMEM((4, 2, 3, 128, WIDE), BF16),
            pltpu.VMEM((4, 128, WIDE), BF16),
            pltpu.VMEM((4, 128, WIDE), BF16),
            pltpu.VMEM((ROWS, WIDE), BF16),
            dma((4,)),
            dma((2, 7)), dma((2, 7)),
            dma((2,)), dma((2,)),
            dma((2, 3)), dma((2, 3)),
            dma((8,)), dma((8,)),
            dma((2,)), dma((2,)),
            dma, dma,
            dma((8,)), dma((8,)), dma((8,)),
            dma((2,)), dma((2,)),
            dma((4,)), dma((4,)),
            dma((4, 2, 3)), dma((4, 2, 3)),
            dma((4,)), dma((4,)),
        ],
        compiler_params=pltpu.CompilerParams(
            collective_id=0, has_side_effects=True, vmem_limit_bytes=58 * 1024 * 1024
        ),
        name="block",
    )(tokens, gain, w_planes, short_taps, taps, skip, w_out)


def per_device(tokens, norm_gain, w_in, short_taps, medium_taps, skip_gain, w_out):
    return block_call(
        tokens,
        norm_gain.reshape(16, 1, WIDE),
        jnp.transpose(w_in, (1, 0, 2)),
        short_taps,
        jnp.transpose(medium_taps),
        skip_gain.reshape(1, CH),
        w_out,
    )


def solution(mesh):
    in_specs = (
        P("seq", "chan"),
        P(),
        P("seq", None, "chan"),
        P(None, None, "chan"),
        P(None, "chan"),
        P("chan"),
        P("chan", None),
    )
    out_specs = P("seq", "chan")
    return jax.shard_map(
        per_device, mesh=mesh, in_specs=in_specs, out_specs=out_specs, check_vma=False
    )
```

```python
import jax
import jax.numpy as jnp
from jax import lax
from jax.experimental import pallas as pl
from jax.experimental.pallas import tpu as pltpu
from jax.sharding import PartitionSpec as P

TAPS = 128
GROUP = 16
EPSILON = 1e-06
MESH = pl.DeviceIdType.MESH
ROWS = 512
WIDE = 512
CH = 256
F32 = jnp.float32
BF16 = jnp.bfloat16
PIECES = 4
PIECE = ROWS // PIECES
CUTS = (0, 112, 240, 368, 512)


def block_kernel(
    x_hbm, gain_ref, w_hbm, short_ref, taps_ref, skip_ref, wo_hbm, out_ref,
    tok, tg, wkv, wq, acc, cs, cr, sq, ss, sr, wo, toep, pj, pe, mix, gate, sb, rb, yb, yr, xres,
    loc, w_send, w_recv, y_send, y_recv, x_send, x_recv, d_send, d_recv, c_send, c_recv, s_send, s_recv,
    o_loc, o_send, o_recv, h_send, h_recv, g_send, g_recv, r_send, r_recv, v_send, v_recv,
):
    s = lax.axis_index("seq")
    c = lax.axis_index("chan")
    y_lo, z = s // 8, s % 8
    y_hi, x, core = c // 8, (c // 2) % 4, c % 2
    f_own = x * 2 + core
    x_right, x_left, x_far = (x + 1) % 4, (x + 3) % 4, (x + 2) % 4
    other = 1 - y_lo

    def at(y_hi_=y_hi, x_=x, core_=core, y_lo_=y_lo, z_=z):
        return (y_lo_ * 8 + z_, y_hi_ * 8 + x_ * 2 + core_)

    right, left = at(x_=x_right), at(x_=x_left)
    up, down = at(z_=(z + 1) % 8), at(z_=(z + 7) % 8)
    twin = at(core_=1 - core)
    mate = at(y_lo_=other)
    opposite = at(y_hi_=1 - y_hi)
    diagonal = at(y_hi_=1 - y_hi, y_lo_=other)
    after, before = ((s + 1) % 16, c), ((s + 15) % 16, c)

    def remote(src, dst, send, recv, device):
        return pltpu.make_async_remote_copy(
            src_ref=src, dst_ref=dst, send_sem=send, recv_sem=recv, device_id=device, device_id_type=MESH
        )

    own_w = []
    for h in range(2):
        rows = pl.ds(h * 256, 256)
        own_w.append(pltpu.make_async_copy(w_hbm.at[pl.ds(1, 2), rows, :], wkv.at[z, h], loc.at[h]))
    for h in range(2):
        rows = pl.ds(h * 256, 256)
        own_w.append(pltpu.make_async_copy(w_hbm.at[0, rows, :], wq.at[z, h], loc.at[2 + h]))
    for cp in own_w:
        cp.start()

    barrier = pltpu.get_barrier_semaphore()
    peers = (right, left, up, down, twin, mate, opposite, diagonal, after, before)
    for peer in peers:
        pl.semaphore_signal(barrier, inc=1, device_id=peer, device_id_type=MESH)
    pl.semaphore_wait(barrier, len(peers))

    def w_slot(phase, direction, distance, half):
        source = (z + 8 - distance) % 8 if direction == 0 else (z + distance) % 8
        return (wkv, wq)[phase].at[source, half]

    def recv_place(direction, k):
        if k == 6:
            return 4, direction
        return k // 2 + 1, k % 2

    def send_place(direction, k):
        if k < 2:
            return 0, k
        if k == 6:
            return 3, direction
        return (k - 2) // 2 + 1, (k - 2) % 2

    def w_copy(phase, direction, k):
        slot = w_slot(phase, direction, *send_place(direction, k))
        return remote(
            slot, slot, w_send.at[phase, direction, k], w_recv.at[phase, direction, k], up if direction == 0 else down
        )

    def w_wait(phase, direction, k):
        slot = w_slot(phase, direction, *recv_place(direction, k))
        remote(slot, slot, w_send.at[phase, direction, k], w_recv.at[phase, direction, k], up).wait_recv()

    def w_step(phase, k):
        for direction in range(2):
            w_wait(phase, direction, k - 2)
            if k < 6:
                w_copy(phase, direction, k).start()
            elif k - 6 == direction:
                w_copy(phase, direction, 6).start()

    for h in range(2):
        own_w[h].wait()
        for direction in range(2):
            w_copy(0, direction, h).start()

    is_home = y_hi == y_lo

    def piece(q):
        return pl.ds(q * PIECE, PIECE)

    def y_copy(d, q):
        return remote(
            x_hbm.at[piece(q), :], tok.at[y_lo, f_own, piece(q), :],
            y_send.at[d, q], y_recv.at[y_lo, q], at(y_lo_=y_hi, y_hi_=d),
        )

    def y_keep(q):
        return pltpu.make_async_copy(x_hbm.at[piece(q), :], tok.at[y_lo, f_own, piece(q), :], loc.at[5 + q])

    for q in range(PIECES):
        for d in range(2):
            stays = jnp.logical_and(is_home, y_hi == d)

            @pl.when(jnp.logical_not(stays))
            def _():
                y_copy(d, q).start()

            @pl.when(stays)
            def _():
                y_keep(q).start()

    def columns(d, core_):
        return wo_hbm.at[:, pl.ds(pl.multiple_of((d * 2 + core_) * WIDE, WIDE), WIDE)]

    def o_keep(d):
        return pltpu.make_async_copy(columns(d, core), wo.at[core, d], o_loc.at[d])

    def o_copy(d):
        return remote(columns(d, 1 - core), wo.at[core, d], o_send.at[d], o_recv.at[d], twin)

    for d in range(8):
        o_copy(d).start()
        o_keep(d).start()
    keep_x = pltpu.make_async_copy(x_hbm, xres, loc.at[4])
    keep_x.start()

    def x_place(direction, k):
        u = direction if k != 1 else 1 - direction
        return u, (x_far if k == 2 else x_left if direction == 0 else x_right)

    def x_copy(direction, k, q):
        if k < 2:
            slot = tok.at[direction if k == 0 else 1 - direction, f_own, piece(q), :]
        else:
            slot = tok.at[direction, (x_left if direction == 0 else x_right) * 2 + core, piece(q), :]
        return remote(
            slot, slot, x_send.at[direction, k, q], x_recv.at[direction, k, q], right if direction == 0 else left
        )

    def x_wait(direction, k, q):
        u, source = x_place(direction, k)
        slot = tok.at[u, source * 2 + core, piece(q), :]
        remote(slot, slot, x_send.at[direction, k, q], x_recv.at[direction, k, q], right).wait_recv()

    places = [(0, x), (1, x)] + [x_place(direction, k) for k in range(3) for direction in range(2)]

    def d_copy(index, q, core_):
        u, source = places[index]
        slot = tok.at[u, source * 2 + core_, piece(q), :]
        return remote(slot, slot, d_send.at[index, q], d_recv.at[index, q], twin)

    def y_arrived(q):
        for u in range(2):
            stays = jnp.logical_and(is_home, y_lo == u)
            slot = tok.at[u, f_own, piece(q), :]

            @pl.when(jnp.logical_not(stays))
            def _():
                remote(slot, slot, y_send.at[0, q], y_recv.at[u, q], right).wait_recv()

            @pl.when(stays)
            def _():
                y_keep(q).wait()

        for k in range(2):
            for direction in range(2):
                x_copy(direction, k, q).start()
        for index in range(2):
            d_copy(index, q, core).start()

    def x_arrived(k, q):
        for direction in range(2):
            x_wait(direction, k, q)
            if k == 0:
                x_copy(direction, 2, q).start()
            d_copy(2 + 2 * k + direction, q, core).start()

    def scaled(index, q, core_):
        u, source = places[index]
        f = source * 2 + core_

        def body(i, carry):
            rows = pl.ds(pl.multiple_of(q * PIECE + i * 64, 64), 64)
            raw = tok[u, f, rows, :].astype(F32)
            gain = gain_ref[pl.ds(y_lo * 8 + f, 1), 0, :]
            tg[u, f, rows, :] = (raw * gain).astype(BF16)
            square = raw * raw
            sq[u, rows, :] += square[:, 0:128] + square[:, 128:256] + square[:, 256:384] + square[:, 384:512]
            return carry

        lax.fori_loop(0, PIECE // 64, body, 0)

    def taken(indices, pieces):
        for index in indices:
            for q in pieces:
                scaled(index, q, core)
                d_copy(index, q, 1 - core).wait_recv()
                scaled(index, q, 1 - core)

    acc[...] = jnp.zeros_like(acc)
    sq[...] = jnp.zeros_like(sq)
    y_arrived(0)
    w_step(0, 2)
    y_arrived(1)
    w_step(0, 3)
    y_arrived(2)
    y_arrived(3)
    x_arrived(0, 0)
    w_step(0, 4)
    x_arrived(0, 1)

    spread = (
        lax.broadcasted_iota(jnp.int32, (TAPS, 2 * TAPS), 0) + lax.broadcasted_iota(jnp.int32, (TAPS, 2 * TAPS), 1)
        == TAPS
    ).astype(F32)
    first = jnp.dot(taps_ref[...], spread, precision=lax.Precision.HIGHEST, preferred_element_type=F32)
    for g in range(16):
        row = jnp.broadcast_to(first[g : g + 1, :], (TAPS, 2 * TAPS))
        matrix = pltpu.roll(row, 0, 1, stride=1, stride_axis=0)
        high = matrix.astype(BF16)
        toep[0, g] = high
        toep[1, g] = (matrix - high.astype(F32)).astype(BF16)

    w_step(0, 5)
    x_arrived(0, 2)
    taken((0, 1), (0, 1))
    w_step(0, 6)
    x_arrived(0, 3)
    taken((0, 1), (2, 3))
    w_step(0, 7)
    for h in range(2):
        own_w[2 + h].wait()
        for direction in range(2):
            w_copy(1, direction, h).start()
    for q in range(PIECES):
        x_arrived(1, q)
        taken((2, 3), (q,))
    for q in range(PIECES):
        taken((4, 5), (q,))
    for q in range(PIECES):
        x_arrived(2, q)
        taken((6, 7), (q,))

    def row_sums(u):
        column = jnp.sum(sq[u], axis=1, keepdims=True)
        return jnp.transpose(jnp.broadcast_to(column, (ROWS, 128)))[0:8, :]

    ss[...] = row_sums(other)
    s_copy = remote(ss, sr, s_send, s_recv, mate)
    s_copy.start()

    def add_kv(u, low, count):
        rows = pl.ds(low, count)

        def body(f, carry):
            lhs0, lhs1 = tg[u, f, rows, 0:256], tg[u, f, rows, 256:512]
            for p in range(2):
                part = jnp.dot(lhs0, wkv[f, 0, p], preferred_element_type=F32)
                part += jnp.dot(lhs1, wkv[f, 1, p], preferred_element_type=F32)
                acc[u, 1 + p, rows, :] += part
            return carry

        lax.fori_loop(0, 8, body, 0)

    def add_q(u, f, low, count):
        rows = pl.ds(low, count)
        part = jnp.dot(tg[u, f, rows, 0:256], wq[f, 0], preferred_element_type=F32)
        part += jnp.dot(tg[u, f, rows, 256:512], wq[f, 1], preferred_element_type=F32)
        return acc[u, 0, rows, :] + part

    def add_q_chunk(f):
        for u in range(2):
            for low in (0, 256):
                acc[u, 0, pl.ds(low, 256), :] = add_q(u, f, low, 256)

    kv_cuts = ((240, 272), (0, 240))

    def c_kv(i):
        rows = pl.ds(*kv_cuts[i])
        planes = pl.ds(1, 2)
        return remote(cs.at[planes, rows, :], cr.at[planes, rows, :], c_send.at[i], c_recv.at[i], mate)

    def c_q(r):
        rows = pl.ds(CUTS[r], CUTS[r + 1] - CUTS[r])
        return remote(cs.at[0, rows, :], cr.at[0, rows, :], c_send.at[2 + r], c_recv.at[2 + r], mate)

    def give_kv(i):
        add_kv(other, *kv_cuts[i])
        rows = pl.ds(*kv_cuts[i])
        for p in (1, 2):
            cs[p, rows, :] = acc[other, p, rows, :].astype(BF16)
        c_kv(i).start()

    def finish(p, low, count):
        rows = pl.ds(low, count)
        factor = sq[0, rows, :]
        factor = jnp.concatenate([factor, factor], axis=1)
        value = acc[y_lo, p, rows, :] + cr[p, rows, :].astype(F32)
        pj[p, pl.ds(16 + low, count), :] = (value * factor).astype(BF16)

    def filtered(p, r):
        extended = pj[p, pl.ds(r * 128, 144), :].astype(F32)
        taps = [short_ref[k, pl.ds(p, 1), :] for k in range(3)]
        return taps[0] * extended[16:144] + taps[1] * extended[15:143] + taps[2] * extended[14:142]

    def make_product(r):
        pe[pl.ds(128 + r * 128, 128), :] = (filtered(1, r) * filtered(2, r)).astype(BF16)

    kv_planes = pl.ds(1, 2)
    halo_kv = [
        remote(pe.at[pl.ds(512, 128), :], pe.at[pl.ds(0, 128), :], h_send.at[0], h_recv.at[0], after),
        remote(pj.at[kv_planes, pl.ds(512, 16), :], pj.at[kv_planes, pl.ds(0, 16), :], h_send.at[1], h_recv.at[1], after),
    ]
    halo_q = remote(pj.at[0, pl.ds(512, 16), :], pj.at[0, pl.ds(0, 16), :], h_send.at[2], h_recv.at[2], after)
    has_after, has_before = s < 15, s > 0

    group_of_lane = lax.broadcasted_iota(jnp.int32, (128, CH), 1) // GROUP

    def make_mixing(r):
        window = pe[pl.ds(r * 128, 256), :]

        def body(g, mixed):
            part = jnp.dot(toep[0, g], window, preferred_element_type=F32)
            part += jnp.dot(toep[1, g], window, preferred_element_type=F32)
            return jnp.where(group_of_lane == g, part, mixed)

        mixed = lax.fori_loop(0, 16, body, jnp.zeros((128, CH), F32), unroll=4)
        product = pe[pl.ds(128 + r * 128, 128), :].astype(F32)
        mix[pl.ds(r * 128, 128), :] = skip_ref[...] * product + mixed

    for direction in range(2):
        w_wait(0, direction, 6)
    give_kv(0)
    w_step(1, 2)
    give_kv(1)
    w_step(1, 3)
    add_kv(y_lo, 240, 272)
    w_step(1, 4)
    add_kv(y_lo, 0, 240)
    s_copy.wait()
    total = row_sums(y_lo) + sr[...]
    factor = lax.rsqrt(total * (1.0 / 8192.0) + EPSILON)
    sq[0] = jnp.transpose(jnp.broadcast_to(factor[0:1, :], (128, ROWS)))

    @pl.when(s == 0)
    def _():
        pe[pl.ds(0, 128), :] = jnp.zeros((128, CH), BF16)
        pj[:, pl.ds(0, 16), :] = jnp.zeros((3, 16, CH), BF16)

    w_step(1, 5)
    c_kv(0).wait_recv()
    for p in (1, 2):
        finish(p, *kv_cuts[0])
    make_product(3)

    @pl.when(has_after)
    def _():
        for cp in halo_kv:
            cp.start()

    make_product(2)
    w_step(1, 6)
    make_mixing(3)
    for distance in (0, 1, 2):
        add_q_chunk((z + distance) % 8)
        if distance:
            add_q_chunk((z + 8 - distance) % 8)
    w_step(1, 7)
    c_kv(1).wait_recv()
    for p in (1, 2):
        finish(p, *kv_cuts[1])
    make_product(1)
    make_mixing(2)
    add_q_chunk((z + 3) % 8)
    add_q_chunk((z + 5) % 8)

    @pl.when(has_before)
    def _():
        for cp in halo_kv:
            cp.wait_recv()

    make_product(0)
    make_mixing(1)
    make_mixing(0)
    for d in range(8):
        o_keep(d).wait()
        remote(wo.at[1 - core, d], wo.at[1 - core, d], o_send.at[d], o_recv.at[d], twin).wait_recv()
    keep_x.wait()

    for direction in range(2):
        w_wait(1, direction, 6)
    f_last = (z + 4) % 8
    for r in (3, 2, 1, 0):
        low, count = CUTS[r], CUTS[r + 1] - CUTS[r]
        cs[0, pl.ds(low, count), :] = add_q(other, f_last, low, count).astype(BF16)
        c_q(r).start()
    for low in (256, 0):
        acc[y_lo, 0, pl.ds(low, 256), :] = add_q(y_lo, f_last, low, 256)

    def g_copy(r):
        place = gate.at[core, pl.ds(r * 128, 128), :]
        return remote(place, place, g_send.at[r], g_recv.at[r], twin)

    def make_gating(r):
        rows = pl.ds(r * 128, 128)
        gate[core, rows, :] = (filtered(0, r) * mix[rows, :]).astype(BF16)
        g_copy(r).start()

    def arrive_q(r):
        c_q(r).wait_recv()
        finish(0, CUTS[r], CUTS[r + 1] - CUTS[r])

    def block(r, x_, y_hi_):
        d = y_hi_ * 4 + x_
        rows = pl.ds(r * 128, 128)
        part = jnp.dot(gate[0, rows, :], wo[0, d], preferred_element_type=F32)
        return part + jnp.dot(gate[1, rows, :], wo[1, d], preferred_element_type=F32)

    def r_copy(r, direction, k):
        return remote(
            sb.at[r, direction, k], rb.at[r, direction, k], r_send.at[r, direction, k], r_recv.at[r, direction, k],
            right if direction == 0 else left,
        )

    def v_copy(r):
        return remote(yb.at[r], yr.at[r], v_send.at[r], v_recv.at[r], opposite)

    nears = (x_right, x_left)

    def send_first(r):
        twin_place = gate.at[1 - core, pl.ds(r * 128, 128), :]
        remote(twin_place, twin_place, g_send.at[r], g_recv.at[r], twin).wait_recv()
        for direction in range(2):
            sb[r, direction, 0] = block(r, x_far, direction).astype(BF16)
            r_copy(r, direction, 0).start()
        for direction in range(2):
            sb[r, direction, 1] = block(r, nears[direction], 1 - direction).astype(BF16)
            r_copy(r, direction, 1).start()

    def send_joined(r):
        for direction in range(2):
            mine = block(r, nears[direction], direction)
            r_copy(r, direction, 0).wait_recv()
            sb[r, direction, 2] = (mine + rb[r, direction, 0].astype(F32)).astype(BF16)
            r_copy(r, direction, 2).start()

    def summed(r, y_hi_):
        mine = block(r, x, y_hi_)
        alone, joined = rb[r, 1 - y_hi_, 1], rb[r, y_hi_, 2]
        return mine + alone.astype(F32) + joined.astype(F32)

    def send_across(r):
        for direction in range(2):
            r_copy(r, direction, 1).wait_recv()
            r_copy(r, direction, 2).wait_recv()
        yb[r] = summed(r, 1 - y_hi).astype(BF16)
        v_copy(r).start()

    def write(r):
        rows = pl.ds(r * 128, 128)
        mine = summed(r, y_hi) + xres[rows, :].astype(F32)
        v_copy(r).wait_recv()
        out_ref[rows, :] = (mine + yr[r].astype(F32)).astype(BF16)

    arrive_q(3)

    @pl.when(has_after)
    def _():
        halo_q.start()

    make_gating(3)
    arrive_q(2)
    make_gating(2)
    send_first(3)
    arrive_q(1)
    make_gating(1)
    send_first(2)
    arrive_q(0)

    @pl.when(has_before)
    def _():
        halo_q.wait_recv()

    make_gating(0)
    send_joined(3)
    send_first(1)
    send_joined(2)
    send_first(0)
    send_across(3)
    send_joined(1)
    send_across(2)
    write(3)
    send_joined(0)
    send_across(1)
    write(2)
    send_across(0)
    write(1)
    write(0)

    for direction in range(2):
        for k in range(7):
            for phase in range(2):
                w_copy(phase, direction, k).wait_send()
        for k in range(3):
            for q in range(PIECES):
                x_copy(direction, k, q).wait_send()
    for d in range(2):

        @pl.when(jnp.logical_not(jnp.logical_and(is_home, y_hi == d)))
        def _():
            for q in range(PIECES):
                y_copy(d, q).wait_send()

    for index in range(8):
        for q in range(PIECES):
            d_copy(index, q, core).wait_send()
    for i in range(2):
        c_kv(i).wait_send()
    for d in range(8):
        o_copy(d).wait_send()
    for r in range(4):
        c_q(r).wait_send()
        g_copy(r).wait_send()
        v_copy(r).wait_send()
        for direction in range(2):
            for k in range(3):
                r_copy(r, direction, k).wait_send()

    @pl.when(has_after)
    def _():
        for cp in halo_kv + [halo_q]:
            cp.wait_send()


def block_call(tokens, gain, w_planes, short_taps, taps, skip, w_out):
    dma = pltpu.SemaphoreType.DMA
    vmem = pl.BlockSpec(memory_space=pltpu.VMEM)
    far = pl.BlockSpec(memory_space=pl.ANY)
    return pl.pallas_call(
        block_kernel,
        out_shape=jax.ShapeDtypeStruct((ROWS, WIDE), BF16),
        in_specs=[far, vmem, far, vmem, vmem, vmem, far],
        out_specs=vmem,
        scratch_shapes=[
            pltpu.VMEM((2, 8, ROWS, WIDE), BF16),
            pltpu.VMEM((2, 8, ROWS, WIDE), BF16),
            pltpu.VMEM((8, 2, 2, 256, CH), BF16),
            pltpu.VMEM((8, 2, 256, CH), BF16),
            pltpu.VMEM((2, 3, ROWS, CH), F32),
            pltpu.VMEM((3, ROWS, CH), BF16),
            pltpu.VMEM((3, ROWS, CH), BF16),
            pltpu.VMEM((2, ROWS, 128), F32),
            pltpu.VMEM((8, ROWS), F32),
            pltpu.VMEM((8, ROWS), F32),
            pltpu.VMEM((2, 8, CH, WIDE), BF16),
            pltpu.VMEM((2, 16, TAPS, 2 * TAPS), BF16),
            pltpu.VMEM((3, 16 + ROWS, CH), BF16),
            pltpu.VMEM((128 + ROWS, CH), BF16),
            pltpu.VMEM((ROWS, CH), F32),
            pltpu.VMEM((2, ROWS, CH), BF16),
            pltpu.VMEM((4, 2, 3, 128, WIDE), BF16),
            pltpu.VMEM((4, 2, 3, 128, WIDE), BF16),
            pltpu.VMEM((4, 128, WIDE), BF16),
            pltpu.VMEM((4, 128, WIDE), BF16),
            pltpu.VMEM((ROWS, WIDE), BF16),
            dma((9,)),
            dma((2, 2, 7)), dma((2, 2, 7)),
            dma((2, PIECES)), dma((2, PIECES)),
            dma((2, 3, PIECES)), dma((2, 3, PIECES)),
            dma((8, PIECES)), dma((8, PIECES)),
            dma((6,)), dma((6,)),
            dma, dma,
            dma((8,)), dma((8,)), dma((8,)),
            dma((3,)), dma((3,)),
            dma((4,)), dma((4,)),
            dma((4, 2, 3)), dma((4, 2, 3)),
            dma((4,)), dma((4,)),
        ],
        compiler_params=pltpu.CompilerParams(
            collective_id=0, has_side_effects=True, vmem_limit_bytes=58 * 1024 * 1024
        ),
        name="block",
    )(tokens, gain, w_planes, short_taps, taps, skip, w_out)


def per_device(tokens, norm_gain, w_in, short_taps, medium_taps, skip_gain, w_out):
    return block_call(
        tokens,
        norm_gain.reshape(16, 1, WIDE),
        jnp.transpose(w_in, (1, 0, 2)),
        short_taps,
        jnp.transpose(medium_taps),
        skip_gain.reshape(1, CH),
        w_out,
    )


def solution(mesh):
    in_specs = (
        P("seq", "chan"),
        P(),
        P("seq", None, "chan"),
        P(None, None, "chan"),
        P(None, "chan"),
        P("chan"),
        P("chan", None),
    )
    out_specs = P("seq", "chan")
    return jax.shard_map(
        per_device, mesh=mesh, in_specs=in_specs, out_specs=out_specs, check_vma=False
    )
```

```python
import jax
import jax.numpy as jnp
from jax import lax
from jax.experimental import pallas as pl
from jax.experimental.pallas import tpu as pltpu
from jax.sharding import PartitionSpec as P

TAPS = 128
GROUP = 16
EPSILON = 1e-06
MESH = pl.DeviceIdType.MESH
ROWS = 512
WIDE = 512
CH = 256
F32 = jnp.float32
BF16 = jnp.bfloat16
PIECES = 4
PIECE = ROWS // PIECES
CHUNKS = 2
CHUNK = ROWS // CHUNKS
CUTS = [0] + [r * CHUNK - 16 for r in range(1, CHUNKS)] + [ROWS]


def block_kernel(
    x_hbm, gain_ref, w_hbm, short_ref, taps_ref, skip_ref, wo_hbm, out_ref,
    tok, tg, wkv, wq, stage, acc, cs, cr, sq, ss, sr, wo, toep, pj, pe, mix, gate, xres,
    loc, w_send, w_recv, y_send, y_recv, f_send, f_recv, x_send, x_recv, d_send, d_recv, c_send, c_recv, s_send, s_recv,
    o_send, o_recv, m_send, m_recv, h_send, h_recv, v_send, v_recv, a_send, a_recv, t_send, t_recv,
):
    s = lax.axis_index("seq")
    c = lax.axis_index("chan")
    y_lo, z = s // 8, s % 8
    y_hi, x, core = c // 8, (c // 2) % 4, c % 2
    f_own = x * 2 + core
    x_right, x_left, x_far = (x + 1) % 4, (x + 3) % 4, (x + 2) % 4
    other = 1 - y_lo

    def at(y_hi_=y_hi, x_=x, core_=core, y_lo_=y_lo, z_=z):
        return (y_lo_ * 8 + z_, y_hi_ * 8 + x_ * 2 + core_)

    right, left = at(x_=x_right), at(x_=x_left)
    up, down = at(z_=(z + 1) % 8), at(z_=(z + 7) % 8)
    twin = at(core_=1 - core)
    mate = at(y_lo_=other)
    opposite = at(y_hi_=1 - y_hi)
    diagonal = at(y_hi_=1 - y_hi, y_lo_=other)
    after, before = ((s + 1) % 16, c), ((s + 15) % 16, c)

    def remote(src, dst, send, recv, device):
        return pltpu.make_async_remote_copy(
            src_ref=src, dst_ref=dst, send_sem=send, recv_sem=recv, device_id=device, device_id_type=MESH
        )

    own_w = []
    for h in range(2):
        rows = pl.ds(h * 256, 256)
        own_w.append(pltpu.make_async_copy(w_hbm.at[pl.ds(1, 2), rows, :], wkv.at[z, h], loc.at[h]))
    for h in range(2):
        rows = pl.ds(h * 256, 256)
        own_w.append(pltpu.make_async_copy(w_hbm.at[0, rows, :], wq.at[z, h], loc.at[2 + h]))
    for cp in own_w:
        cp.start()

    barrier = pltpu.get_barrier_semaphore()
    def w_out_peers(y_hi_, y_lo_, xs):
        return [at(y_hi_=y_hi_, y_lo_=y_lo_, x_=x_, core_=k) for x_ in xs for k in range(2)]

    o_peers = (
        w_out_peers(y_hi, y_lo, (x_right, x_left))
        + w_out_peers(1 - y_hi, other, (x_right, x_left))
        + w_out_peers(y_hi, y_lo, (x_far,))
        + w_out_peers(1 - y_hi, other, (x_far, x))
        + [twin]
    )
    peers = o_peers + [up, down, mate, opposite, after, before]
    for peer in peers:
        pl.semaphore_signal(barrier, inc=1, device_id=peer, device_id_type=MESH)
    pl.semaphore_wait(barrier, len(peers))

    def w_slot(phase, direction, distance, half):
        source = (z + 8 - distance) % 8 if direction == 0 else (z + distance) % 8
        return (wkv, wq)[phase].at[source, half]

    def recv_place(direction, k):
        if k == 6:
            return 4, direction
        return k // 2 + 1, k % 2

    def send_place(direction, k):
        if k < 2:
            return 0, k
        if k == 6:
            return 3, direction
        return (k - 2) // 2 + 1, (k - 2) % 2

    def w_copy(phase, direction, k):
        slot = w_slot(phase, direction, *send_place(direction, k))
        return remote(
            slot, slot, w_send.at[phase, direction, k], w_recv.at[phase, direction, k], up if direction == 0 else down
        )

    def w_wait(phase, direction, k):
        slot = w_slot(phase, direction, *recv_place(direction, k))
        remote(slot, slot, w_send.at[phase, direction, k], w_recv.at[phase, direction, k], up).wait_recv()

    def w_step(phase, k):
        for direction in range(2):
            w_wait(phase, direction, k - 2)
            if k < 6:
                w_copy(phase, direction, k).start()
            elif k - 6 == direction:
                w_copy(phase, direction, 6).start()

    for h in range(2):
        own_w[h].wait()
        for direction in range(2):
            w_copy(0, direction, h).start()

    is_home = y_hi == y_lo

    def piece(q):
        return pl.ds(q * PIECE, PIECE)

    def y_copy(d, q):
        return remote(
            x_hbm.at[piece(q), :], tok.at[y_lo, f_own, piece(q), :],
            y_send.at[d, q], y_recv.at[y_lo, q], at(y_lo_=y_hi, y_hi_=d),
        )

    def y_keep(q):
        return pltpu.make_async_copy(x_hbm.at[piece(q), :], tok.at[y_lo, f_own, piece(q), :], loc.at[5 + q])

    SHARED = (8, 9, 10, 11)
    odd = z % 2
    buddy = at(z_=z + 1 - 2 * odd)

    def o_rows(i, half):
        return pl.ds(pl.multiple_of(half * 128, 128), 128) if i in SHARED else pl.ds(0, 256)

    def o_copy(i):
        device = o_peers[i]
        rows = o_rows(i, odd)
        there = wo_hbm.at[rows, pl.ds(pl.multiple_of(device[1] * WIDE, WIDE), WIDE)]
        return remote(there, wo.at[c, rows, :], o_send.at[i], o_recv.at[c], device)

    def o_wait(i):
        source = o_peers[i][1]
        slot = wo.at[source, o_rows(i, odd), :]
        remote(slot, slot, o_send.at[i], o_recv.at[source], twin).wait_recv()

    def m_copy(i):
        slot = wo.at[o_peers[i][1], o_rows(i, odd), :]
        return remote(slot, slot, m_send.at[i], m_recv.at[i], buddy)

    def m_wait(i):
        slot = wo.at[o_peers[i][1], o_rows(i, 1 - odd), :]
        remote(slot, slot, m_send.at[i], m_recv.at[i], buddy).wait_recv()

    o_keep = pltpu.make_async_copy(wo_hbm.at[:, pl.ds(pl.multiple_of(c * WIDE, WIDE), WIDE)], wo.at[c], loc.at[9])

    def f_copy(q):
        return remote(x_hbm.at[piece(q), :], stage.at[piece(q), :], f_send.at[q], f_recv.at[q], diagonal)

    def f_pass(q):
        return remote(
            stage.at[piece(q), :], tok.at[other, f_own, piece(q), :], y_send.at[1 - y_hi, q], y_recv.at[other, q], mate
        )

    for q in range(PIECES):
        for d in range(2):
            stays = jnp.logical_and(is_home, y_hi == d)

            @pl.when(jnp.logical_not(is_home))
            def _():
                y_copy(d, q).start()

            @pl.when(stays)
            def _():
                y_keep(q).start()
                f_copy(q).start()

    for i in (8, 9, 10, 11):
        o_copy(i).start()
    o_copy(14).start()
    o_keep.start()
    keep_x = pltpu.make_async_copy(x_hbm, xres, loc.at[4])
    keep_x.start()

    def x_place(direction, k):
        u = direction if k != 1 else 1 - direction
        return u, (x_far if k == 2 else x_left if direction == 0 else x_right)

    def x_copy(direction, k, q):
        if k < 2:
            slot = tok.at[direction if k == 0 else 1 - direction, f_own, piece(q), :]
        else:
            slot = tok.at[direction, (x_left if direction == 0 else x_right) * 2 + core, piece(q), :]
        return remote(
            slot, slot, x_send.at[direction, k, q], x_recv.at[direction, k, q], right if direction == 0 else left
        )

    def x_wait(direction, k, q):
        u, source = x_place(direction, k)
        slot = tok.at[u, source * 2 + core, piece(q), :]
        remote(slot, slot, x_send.at[direction, k, q], x_recv.at[direction, k, q], right).wait_recv()

    places = [(0, x), (1, x)] + [x_place(direction, k) for k in range(3) for direction in range(2)]

    def d_copy(index, q, core_):
        u, source = places[index]
        slot = tok.at[u, source * 2 + core_, piece(q), :]
        return remote(slot, slot, d_send.at[index, q], d_recv.at[index, q], twin)

    def send_own(u, q):
        for direction in range(2):
            k = 1 - u if direction else u
            slot = tok.at[u, f_own, piece(q), :]
            remote(
                slot, slot, x_send.at[direction, k, q], x_recv.at[direction, k, q], right if direction == 0 else left
            ).start()
        slot = tok.at[u, f_own, piece(q), :]
        remote(slot, slot, d_send.at[u, q], d_recv.at[u, q], twin).start()

    def y_arrived(q):
        slot = tok.at[other, f_own, piece(q), :]
        remote(slot, slot, y_send.at[0, q], y_recv.at[other, q], right).wait_recv()
        send_own(other, q)

    def y_far_arrived(q):
        slot = tok.at[y_lo, f_own, piece(q), :]

        @pl.when(is_home)
        def _():
            remote(stage.at[piece(q), :], stage.at[piece(q), :], f_send.at[q], f_recv.at[q], right).wait_recv()
            f_pass(q).start()
            y_keep(q).wait()

        @pl.when(jnp.logical_not(is_home))
        def _():
            remote(slot, slot, y_send.at[0, q], y_recv.at[y_lo, q], right).wait_recv()

        send_own(y_lo, q)

    def x_arrived(k, q):
        for direction in range(2):
            x_wait(direction, k, q)
            if k == 0:
                x_copy(direction, 2, q).start()
            d_copy(2 + 2 * k + direction, q, core).start()

    def scaled(index, q, core_):
        u, source = places[index]
        f = source * 2 + core_

        def body(i, carry):
            rows = pl.ds(pl.multiple_of(q * PIECE + i * 64, 64), 64)
            raw = tok[u, f, rows, :].astype(F32)
            gain = gain_ref[pl.ds(y_lo * 8 + f, 1), 0, :]
            tg[u, f, rows, :] = (raw * gain).astype(BF16)
            square = raw * raw
            sq[u, rows, :] += square[:, 0:128] + square[:, 128:256] + square[:, 256:384] + square[:, 384:512]
            return carry

        lax.fori_loop(0, PIECE // 64, body, 0)

    def taken(indices, pieces):
        for index in indices:
            for q in pieces:
                scaled(index, q, core)
                d_copy(index, q, 1 - core).wait_recv()
                scaled(index, q, 1 - core)

    acc[...] = jnp.zeros_like(acc)
    sq[...] = jnp.zeros_like(sq)
    y_arrived(0)
    w_step(0, 2)
    y_far_arrived(0)
    y_arrived(1)
    y_far_arrived(1)
    w_step(0, 3)
    y_arrived(2)
    y_far_arrived(2)
    y_arrived(3)
    y_far_arrived(3)
    x_arrived(0, 0)
    w_step(0, 4)
    x_arrived(0, 1)

    spread = (
        lax.broadcasted_iota(jnp.int32, (TAPS, 2 * TAPS), 0) + lax.broadcasted_iota(jnp.int32, (TAPS, 2 * TAPS), 1)
        == TAPS
    ).astype(F32)
    first = jnp.dot(taps_ref[...], spread, precision=lax.Precision.HIGHEST, preferred_element_type=F32)
    for g in range(16):
        row = jnp.broadcast_to(first[g : g + 1, :], (TAPS, 2 * TAPS))
        matrix = pltpu.roll(row, 0, 1, stride=1, stride_axis=0)
        high = matrix.astype(BF16)
        toep[0, g] = high
        toep[1, g] = (matrix - high.astype(F32)).astype(BF16)

    w_step(0, 5)
    x_arrived(0, 2)
    taken((0, 1), range(PIECES // 2))
    w_step(0, 6)
    x_arrived(0, 3)
    for i in (0, 2, 1, 3, 4, 6, 5, 7, 12, 13):
        o_copy(i).start()
    taken((0, 1), range(PIECES // 2, PIECES))
    w_step(0, 7)
    for h in range(2):
        own_w[2 + h].wait()
        for direction in range(2):
            w_copy(1, direction, h).start()
    for q in range(PIECES):
        x_arrived(1, q)
        taken((2, 3), (q,))
    taken((4, 5), range(PIECES))
    w_step(1, 2)
    x_arrived(2, 0)
    x_arrived(2, 1)
    taken((6, 7), (0, 1))
    w_step(1, 3)
    x_arrived(2, 2)
    x_arrived(2, 3)
    taken((6, 7), (2, 3))

    def row_sums(u):
        column = jnp.sum(sq[u], axis=1, keepdims=True)
        return jnp.transpose(jnp.broadcast_to(column, (ROWS, 128)))[0:8, :]

    ss[...] = row_sums(other)
    s_copy = remote(ss, sr, s_send, s_recv, mate)
    s_copy.start()

    def add_kv(u, low, count):
        rows = pl.ds(low, count)

        def body(f, carry):
            lhs0, lhs1 = tg[u, f, rows, 0:256], tg[u, f, rows, 256:512]
            for p in range(2):
                part = jnp.dot(lhs0, wkv[f, 0, p], preferred_element_type=F32)
                part += jnp.dot(lhs1, wkv[f, 1, p], preferred_element_type=F32)
                acc[u, 1 + p, rows, :] += part
            return carry

        lax.fori_loop(0, 8, body, 0)

    def add_q(u, f, low, count):
        rows = pl.ds(low, count)
        part = jnp.dot(tg[u, f, rows, 0:256], wq[f, 0], preferred_element_type=F32)
        part += jnp.dot(tg[u, f, rows, 256:512], wq[f, 1], preferred_element_type=F32)
        return acc[u, 0, rows, :] + part

    def add_q_chunk(f):
        for u in range(2):
            for low in (0, 256):
                acc[u, 0, pl.ds(low, 256), :] = add_q(u, f, low, 256)

    kv_cuts = ((240, 272), (0, 240))

    def c_kv(i):
        rows = pl.ds(*kv_cuts[i])
        planes = pl.ds(1, 2)
        return remote(cs.at[planes, rows, :], cr.at[planes, rows, :], c_send.at[i], c_recv.at[i], mate)

    def c_q(r):
        rows = pl.ds(CUTS[r], CUTS[r + 1] - CUTS[r])
        return remote(cs.at[0, rows, :], cr.at[0, rows, :], c_send.at[2 + r], c_recv.at[2 + r], mate)

    def give_kv(i):
        add_kv(other, *kv_cuts[i])
        rows = pl.ds(*kv_cuts[i])
        for p in (1, 2):
            cs[p, rows, :] = acc[other, p, rows, :].astype(BF16)
        c_kv(i).start()

    def finish(p, low, count):
        rows = pl.ds(low, count)
        factor = sq[0, rows, :]
        factor = jnp.concatenate([factor, factor], axis=1)
        value = acc[y_lo, p, rows, :] + cr[p, rows, :].astype(F32)
        pj[p, pl.ds(16 + low, count), :] = (value * factor).astype(BF16)

    def filtered(p, low, n):
        extended = pj[p, pl.ds(low, n + 16), :].astype(F32)
        taps = [short_ref[k, pl.ds(p, 1), :] for k in range(3)]
        return taps[0] * extended[16 : n + 16] + taps[1] * extended[15 : n + 15] + taps[2] * extended[14 : n + 14]

    def make_product(r):
        pe[pl.ds(128 + r * 128, 128), :] = (filtered(1, r * 128, 128) * filtered(2, r * 128, 128)).astype(BF16)

    kv_planes = pl.ds(1, 2)
    halo_kv = [
        remote(pe.at[pl.ds(512, 128), :], pe.at[pl.ds(0, 128), :], h_send.at[0], h_recv.at[0], after),
        remote(pj.at[kv_planes, pl.ds(512, 16), :], pj.at[kv_planes, pl.ds(0, 16), :], h_send.at[1], h_recv.at[1], after),
    ]
    halo_q = remote(pj.at[0, pl.ds(512, 16), :], pj.at[0, pl.ds(0, 16), :], h_send.at[2], h_recv.at[2], after)
    has_after, has_before = s < 15, s > 0

    group_of_lane = lax.broadcasted_iota(jnp.int32, (128, CH), 1) // GROUP

    def make_mixing(r):
        window = pe[pl.ds(r * 128, 256), :]

        def body(g, mixed):
            part = jnp.dot(toep[0, g], window, preferred_element_type=F32)
            part += jnp.dot(toep[1, g], window, preferred_element_type=F32)
            return jnp.where(group_of_lane == g, part, mixed)

        mixed = lax.fori_loop(0, 16, body, jnp.zeros((128, CH), F32), unroll=4)
        product = pe[pl.ds(128 + r * 128, 128), :].astype(F32)
        mix[pl.ds(r * 128, 128), :] = skip_ref[...] * product + mixed

    for direction in range(2):
        w_wait(0, direction, 6)
    give_kv(0)
    w_step(1, 4)
    give_kv(1)
    add_kv(y_lo, 240, 272)
    w_step(1, 5)
    add_kv(y_lo, 0, 240)
    w_step(1, 6)
    s_copy.wait()
    total = row_sums(y_lo) + sr[...]
    factor = lax.rsqrt(total * (1.0 / 8192.0) + EPSILON)
    sq[0] = jnp.transpose(jnp.broadcast_to(factor[0:1, :], (128, ROWS)))

    @pl.when(s == 0)
    def _():
        pe[pl.ds(0, 128), :] = jnp.zeros((128, CH), BF16)
        pj[:, pl.ds(0, 16), :] = jnp.zeros((3, 16, CH), BF16)

    c_kv(0).wait_recv()
    for p in (1, 2):
        finish(p, *kv_cuts[0])
    make_product(3)

    @pl.when(has_after)
    def _():
        for cp in halo_kv:
            cp.start()

    make_product(2)
    w_step(1, 7)
    make_mixing(3)
    for distance in (0, 1, 2):
        add_q_chunk((z + distance) % 8)
        if distance:
            add_q_chunk((z + 8 - distance) % 8)
    c_kv(1).wait_recv()
    for p in (1, 2):
        finish(p, *kv_cuts[1])
    make_product(1)
    make_mixing(2)
    add_q_chunk((z + 3) % 8)
    add_q_chunk((z + 5) % 8)

    @pl.when(has_before)
    def _():
        for cp in halo_kv:
            cp.wait_recv()

    make_product(0)
    make_mixing(1)
    make_mixing(0)
    o_keep.wait()
    keep_x.wait()

    for direction in range(2):
        w_wait(1, direction, 6)
    f_last = (z + 4) % 8
    order = range(CHUNKS - 1, -1, -1)
    for r in order:
        low, count = CUTS[r], CUTS[r + 1] - CUTS[r]
        cs[0, pl.ds(low, count), :] = add_q(other, f_last, low, count).astype(BF16)
        c_q(r).start()
    for i in SHARED:
        o_wait(i)
        m_copy(i).start()
    for low in (256, 0):
        acc[y_lo, 0, pl.ds(low, 256), :] = add_q(y_lo, f_last, low, 256)

    held = [(y_hi, x), (1 - y_hi, x)]
    for y_hi_ in (y_hi, 1 - y_hi):
        held += [(y_hi_, x_left), (y_hi_, x_right)]
    held += [(y_hi, x_far), (1 - y_hi, x_far)]

    def part_of(index, core_, r):
        y_hi_, x_ = held[index]
        return gate.at[y_hi_ * 8 + x_ * 2 + core_, pl.ds(r * CHUNK, CHUNK), :]

    def t_copy(index, r):
        place = part_of(index, core, r)
        return remote(place, place, t_send.at[r, index], t_recv.at[r, index], twin)

    def v_copy(r):
        place = part_of(0, core, r)
        return remote(place, place, v_send.at[r], v_recv.at[r], opposite)

    def a_copy(direction, k, r):
        index = k if k < 2 else 2 if direction == 0 else 5
        place = part_of(index, core, r)
        return remote(
            place, place, a_send.at[r, direction, k], a_recv.at[r, direction, k], right if direction == 0 else left
        )

    def a_arrived(k, r):
        for direction in range(2):
            index = 2 + 2 * k + direction
            place = part_of(index, core, r)
            remote(place, place, a_send.at[r, direction, k], a_recv.at[r, direction, k], right).wait_recv()
            if k == direction:
                a_copy(direction, 2, r).start()
            t_copy(index, r).start()

    def v_arrived(r):
        place = part_of(1, core, r)
        remote(place, place, v_send.at[r], v_recv.at[r], opposite).wait_recv()
        for direction in range(2):
            a_copy(direction, 1, r).start()
        t_copy(1, r).start()

    def make_gating(r):
        rows = pl.ds(r * CHUNK, CHUNK)
        gate[c, rows, :] = (filtered(0, r * CHUNK, CHUNK) * mix[rows, :]).astype(BF16)
        v_copy(r).start()
        for direction in range(2):
            a_copy(direction, 0, r).start()
        t_copy(0, r).start()

    def arrive_q(r):
        c_q(r).wait_recv()
        finish(0, CUTS[r], CUTS[r + 1] - CUTS[r])

    def write(r):
        for index in range(8):
            place = part_of(index, 1 - core, r)
            remote(place, place, t_send.at[r, index], t_recv.at[r, index], twin).wait_recv()

        def body(half, carry):
            rows = pl.ds(r * CHUNK, CHUNK)
            columns = pl.ds(pl.multiple_of(half * 256, 256), 256)
            total = xres[rows, columns].astype(F32)
            for i in range(16):
                total += jnp.dot(gate[i, rows, :], wo[i, :, columns], preferred_element_type=F32)
            out_ref[rows, columns] = total.astype(BF16)
            return carry

        lax.fori_loop(0, 2, body, 0)

    for r in order:
        arrive_q(r)
        if r == CHUNKS - 1:

            @pl.when(has_after)
            def _():
                halo_q.start()

        if r == 0:

            @pl.when(has_before)
            def _():
                halo_q.wait_recv()

        make_gating(r)
    for r in order:
        v_arrived(r)
        a_arrived(0, r)
    for i in range(15):
        if i not in SHARED:
            o_wait(i)
    for i in SHARED:
        m_wait(i)
    for r in order:
        a_arrived(1, r)
    for r in order:
        a_arrived(2, r)
        write(r)

    for direction in range(2):
        for k in range(7):
            for phase in range(2):
                w_copy(phase, direction, k).wait_send()
        for k in range(3):
            for q in range(PIECES):
                x_copy(direction, k, q).wait_send()
    @pl.when(jnp.logical_not(is_home))
    def _():
        for d in range(2):
            for q in range(PIECES):
                y_copy(d, q).wait_send()

    @pl.when(is_home)
    def _():
        for q in range(PIECES):
            f_copy(q).wait_send()
            f_pass(q).wait_send()

    for index in range(8):
        for q in range(PIECES):
            d_copy(index, q, core).wait_send()
    for i in range(2):
        c_kv(i).wait_send()
    for i in range(15):
        o_copy(i).wait_send()
    for i in SHARED:
        m_copy(i).wait_send()
    for r in range(CHUNKS):
        c_q(r).wait_send()
        v_copy(r).wait_send()
        for index in range(8):
            t_copy(index, r).wait_send()
        for direction in range(2):
            for k in range(3):
                a_copy(direction, k, r).wait_send()

    @pl.when(has_after)
    def _():
        for cp in halo_kv + [halo_q]:
            cp.wait_send()


def block_call(tokens, gain, w_planes, short_taps, taps, skip, w_out):
    dma = pltpu.SemaphoreType.DMA
    vmem = pl.BlockSpec(memory_space=pltpu.VMEM)
    far = pl.BlockSpec(memory_space=pl.ANY)
    return pl.pallas_call(
        block_kernel,
        out_shape=jax.ShapeDtypeStruct((ROWS, WIDE), BF16),
        in_specs=[far, vmem, far, vmem, vmem, vmem, far],
        out_specs=vmem,
        scratch_shapes=[
            pltpu.VMEM((2, 8, ROWS, WIDE), BF16),
            pltpu.VMEM((2, 8, ROWS, WIDE), BF16),
            pltpu.VMEM((8, 2, 2, 256, CH), BF16),
            pltpu.VMEM((8, 2, 256, CH), BF16),
            pltpu.VMEM((ROWS, WIDE), BF16),
            pltpu.VMEM((2, 3, ROWS, CH), F32),
            pltpu.VMEM((3, ROWS, CH), BF16),
            pltpu.VMEM((3, ROWS, CH), BF16),
            pltpu.VMEM((2, ROWS, 128), F32),
            pltpu.VMEM((8, ROWS), F32),
            pltpu.VMEM((8, ROWS), F32),
            pltpu.VMEM((16, CH, WIDE), BF16),
            pltpu.VMEM((2, 16, TAPS, 2 * TAPS), BF16),
            pltpu.VMEM((3, 16 + ROWS, CH), BF16),
            pltpu.VMEM((128 + ROWS, CH), BF16),
            pltpu.VMEM((ROWS, CH), F32),
            pltpu.VMEM((16, ROWS, CH), BF16),
            pltpu.VMEM((ROWS, WIDE), BF16),
            dma((10,)),
            dma((2, 2, 7)), dma((2, 2, 7)),
            dma((2, PIECES)), dma((2, PIECES)),
            dma((PIECES,)), dma((PIECES,)),
            dma((2, 3, PIECES)), dma((2, 3, PIECES)),
            dma((8, PIECES)), dma((8, PIECES)),
            dma((6,)), dma((6,)),
            dma, dma,
            dma((15,)), dma((16,)),
            dma((12,)), dma((12,)),
            dma((3,)), dma((3,)),
            dma((CHUNKS,)), dma((CHUNKS,)),
            dma((CHUNKS, 2, 3)), dma((CHUNKS, 2, 3)),
            dma((CHUNKS, 8)), dma((CHUNKS, 8)),
        ],
        compiler_params=pltpu.CompilerParams(
            collective_id=0, has_side_effects=True, vmem_limit_bytes=58 * 1024 * 1024
        ),
        name="block",
    )(tokens, gain, w_planes, short_taps, taps, skip, w_out)


def per_device(tokens, norm_gain, w_in, short_taps, medium_taps, skip_gain, w_out):
    return block_call(
        tokens,
        norm_gain.reshape(16, 1, WIDE),
        jnp.transpose(w_in, (1, 0, 2)),
        short_taps,
        jnp.transpose(medium_taps),
        skip_gain.reshape(1, CH),
        w_out,
    )


def solution(mesh):
    in_specs = (
        P("seq", "chan"),
        P(),
        P("seq", None, "chan"),
        P(None, None, "chan"),
        P(None, "chan"),
        P("chan"),
        P("chan", None),
    )
    out_specs = P("seq", "chan")
    return jax.shard_map(
        per_device, mesh=mesh, in_specs=in_specs, out_specs=out_specs, check_vma=False
    )
```

```python
import jax
import jax.numpy as jnp
from jax import lax
from jax.experimental import pallas as pl
from jax.experimental.pallas import tpu as pltpu
from jax.sharding import PartitionSpec as P

TAPS = 128
GROUP = 16
EPSILON = 1e-06
MESH = pl.DeviceIdType.MESH
ROWS = 512
WIDE = 512
CH = 256
F32 = jnp.float32
BF16 = jnp.bfloat16
PIECES = 4
PIECE = ROWS // PIECES
CHUNKS = 2
CHUNK = ROWS // CHUNKS
CUTS = [0] + [r * CHUNK - 16 for r in range(1, CHUNKS)] + [ROWS]


def block_kernel(
    x_hbm, gain_ref, w_hbm, short_ref, taps_ref, skip_ref, wo_hbm, out_ref,
    tok, tg, wkv, wq, stage, acc, cs, cr, sq, ss, sr, wo, toep, pj, pe, mix, gate, xres,
    loc, w_send, w_recv, y_send, y_recv, f_send, f_recv, x_send, x_recv, d_send, d_recv, c_send, c_recv, s_send, s_recv,
    o_send, o_recv, m_send, m_recv, h_send, h_recv, v_send, v_recv, a_send, a_recv, t_send, t_recv,
):
    s = lax.axis_index("seq")
    c = lax.axis_index("chan")
    y_lo, z = s // 8, s % 8
    y_hi, x, core = c // 8, (c // 2) % 4, c % 2
    f_own = x * 2 + core
    x_right, x_left, x_far = (x + 1) % 4, (x + 3) % 4, (x + 2) % 4
    other = 1 - y_lo

    def at(y_hi_=y_hi, x_=x, core_=core, y_lo_=y_lo, z_=z):
        return (y_lo_ * 8 + z_, y_hi_ * 8 + x_ * 2 + core_)

    right, left = at(x_=x_right), at(x_=x_left)
    up, down = at(z_=(z + 1) % 8), at(z_=(z + 7) % 8)
    twin = at(core_=1 - core)
    mate = at(y_lo_=other)
    opposite = at(y_hi_=1 - y_hi)
    diagonal = at(y_hi_=1 - y_hi, y_lo_=other)
    after, before = ((s + 1) % 16, c), ((s + 15) % 16, c)

    def remote(src, dst, send, recv, device):
        return pltpu.make_async_remote_copy(
            src_ref=src, dst_ref=dst, send_sem=send, recv_sem=recv, device_id=device, device_id_type=MESH
        )

    own_w = []
    for h in range(2):
        rows = pl.ds(h * 256, 256)
        own_w.append(pltpu.make_async_copy(w_hbm.at[pl.ds(1, 2), rows, :], wkv.at[z, h], loc.at[h]))
    for h in range(2):
        rows = pl.ds(h * 256, 256)
        own_w.append(pltpu.make_async_copy(w_hbm.at[0, rows, :], wq.at[z, h], loc.at[2 + h]))
    for cp in own_w:
        cp.start()

    barrier = pltpu.get_barrier_semaphore()
    def w_out_peers(y_hi_, y_lo_, xs):
        return [at(y_hi_=y_hi_, y_lo_=y_lo_, x_=x_, core_=k) for x_ in xs for k in range(2)]

    o_peers = (
        w_out_peers(y_hi, y_lo, (x_right, x_left))
        + w_out_peers(1 - y_hi, other, (x_right, x_left))
        + w_out_peers(y_hi, y_lo, (x_far,))
        + w_out_peers(1 - y_hi, other, (x_far, x))
        + [twin]
    )
    peers = o_peers + [up, down, mate, opposite, after, before]
    for peer in peers:
        pl.semaphore_signal(barrier, inc=1, device_id=peer, device_id_type=MESH)
    pl.semaphore_wait(barrier, len(peers))

    def w_slot(phase, direction, distance, half):
        source = (z + 8 - distance) % 8 if direction == 0 else (z + distance) % 8
        return (wkv, wq)[phase].at[source, half]

    def recv_place(direction, k):
        if k == 6:
            return 4, direction
        return k // 2 + 1, k % 2

    def send_place(direction, k):
        if k < 2:
            return 0, k
        if k == 6:
            return 3, direction
        return (k - 2) // 2 + 1, (k - 2) % 2

    def w_copy(phase, direction, k):
        slot = w_slot(phase, direction, *send_place(direction, k))
        return remote(
            slot, slot, w_send.at[phase, direction, k], w_recv.at[phase, direction, k], up if direction == 0 else down
        )

    def w_wait(phase, direction, k):
        slot = w_slot(phase, direction, *recv_place(direction, k))
        remote(slot, slot, w_send.at[phase, direction, k], w_recv.at[phase, direction, k], up).wait_recv()

    def w_step(phase, k):
        for direction in range(2):
            w_wait(phase, direction, k - 2)
            if k < 6:
                w_copy(phase, direction, k).start()
            elif k - 6 == direction:
                w_copy(phase, direction, 6).start()

    for h in range(2):
        own_w[h].wait()
        for direction in range(2):
            w_copy(0, direction, h).start()

    is_home = y_hi == y_lo

    def piece(q):
        return pl.ds(q * PIECE, PIECE)

    def y_copy(d, q):
        return remote(
            x_hbm.at[piece(q), :], tok.at[y_lo, f_own, piece(q), :],
            y_send.at[d, q], y_recv.at[y_lo, q], at(y_lo_=y_hi, y_hi_=d),
        )

    def y_keep(q):
        return pltpu.make_async_copy(x_hbm.at[piece(q), :], tok.at[y_lo, f_own, piece(q), :], loc.at[5 + q])

    SHARED = (8, 9, 10, 11)
    odd = z % 2
    buddy = at(z_=z + 1 - 2 * odd)

    def o_rows(i, half):
        return pl.ds(pl.multiple_of(half * 128, 128), 128) if i in SHARED else pl.ds(0, 256)

    def o_copy(i):
        device = o_peers[i]
        rows = o_rows(i, odd)
        there = wo_hbm.at[rows, pl.ds(pl.multiple_of(device[1] * WIDE, WIDE), WIDE)]
        return remote(there, wo.at[c, rows, :], o_send.at[i], o_recv.at[c], device)

    def o_wait(i):
        source = o_peers[i][1]
        slot = wo.at[source, o_rows(i, odd), :]
        remote(slot, slot, o_send.at[i], o_recv.at[source], twin).wait_recv()

    def m_copy(i):
        slot = wo.at[o_peers[i][1], o_rows(i, odd), :]
        return remote(slot, slot, m_send.at[i], m_recv.at[i], buddy)

    def m_wait(i):
        slot = wo.at[o_peers[i][1], o_rows(i, 1 - odd), :]
        remote(slot, slot, m_send.at[i], m_recv.at[i], buddy).wait_recv()

    o_keep = pltpu.make_async_copy(wo_hbm.at[:, pl.ds(pl.multiple_of(c * WIDE, WIDE), WIDE)], wo.at[c], loc.at[9])

    def f_copy(q):
        return remote(x_hbm.at[piece(q), :], stage.at[piece(q), :], f_send.at[q], f_recv.at[q], diagonal)

    def f_pass(q):
        return remote(
            stage.at[piece(q), :], tok.at[other, f_own, piece(q), :], y_send.at[1 - y_hi, q], y_recv.at[other, q], mate
        )

    for q in range(PIECES):
        for d in range(2):
            stays = jnp.logical_and(is_home, y_hi == d)

            @pl.when(jnp.logical_not(is_home))
            def _():
                y_copy(d, q).start()

            @pl.when(stays)
            def _():
                y_keep(q).start()
                f_copy(q).start()

    for i in (8, 9, 10, 11):
        o_copy(i).start()
    o_copy(14).start()
    o_keep.start()
    keep_x = pltpu.make_async_copy(x_hbm, xres, loc.at[4])
    keep_x.start()

    def x_place(direction, k):
        u = direction if k != 1 else 1 - direction
        return u, (x_far if k == 2 else x_left if direction == 0 else x_right)

    def x_copy(direction, k, q):
        if k < 2:
            slot = tok.at[direction if k == 0 else 1 - direction, f_own, piece(q), :]
        else:
            slot = tok.at[direction, (x_left if direction == 0 else x_right) * 2 + core, piece(q), :]
        return remote(
            slot, slot, x_send.at[direction, k, q], x_recv.at[direction, k, q], right if direction == 0 else left
        )

    def x_wait(direction, k, q):
        u, source = x_place(direction, k)
        slot = tok.at[u, source * 2 + core, piece(q), :]
        remote(slot, slot, x_send.at[direction, k, q], x_recv.at[direction, k, q], right).wait_recv()

    places = [(0, x), (1, x)] + [x_place(direction, k) for k in range(3) for direction in range(2)]

    def d_copy(index, q, core_):
        u, source = places[index]
        slot = tok.at[u, source * 2 + core_, piece(q), :]
        return remote(slot, slot, d_send.at[index, q], d_recv.at[index, q], twin)

    def send_own(u, q):
        for direction in range(2):
            k = 1 - u if direction else u
            slot = tok.at[u, f_own, piece(q), :]
            remote(
                slot, slot, x_send.at[direction, k, q], x_recv.at[direction, k, q], right if direction == 0 else left
            ).start()
        slot = tok.at[u, f_own, piece(q), :]
        remote(slot, slot, d_send.at[u, q], d_recv.at[u, q], twin).start()

    def y_arrived(q):
        slot = tok.at[other, f_own, piece(q), :]
        remote(slot, slot, y_send.at[0, q], y_recv.at[other, q], right).wait_recv()
        send_own(other, q)

    def y_far_arrived(q):
        slot = tok.at[y_lo, f_own, piece(q), :]

        @pl.when(is_home)
        def _():
            remote(stage.at[piece(q), :], stage.at[piece(q), :], f_send.at[q], f_recv.at[q], right).wait_recv()
            f_pass(q).start()
            y_keep(q).wait()

        @pl.when(jnp.logical_not(is_home))
        def _():
            remote(slot, slot, y_send.at[0, q], y_recv.at[y_lo, q], right).wait_recv()

        send_own(y_lo, q)

    def x_arrived(k, q):
        for direction in range(2):
            x_wait(direction, k, q)
            if k == 0:
                x_copy(direction, 2, q).start()
            d_copy(2 + 2 * k + direction, q, core).start()

    def scaled(index, q, core_):
        u, source = places[index]
        f = source * 2 + core_

        def body(i, carry):
            rows = pl.ds(pl.multiple_of(q * PIECE + i * 64, 64), 64)
            raw = tok[u, f, rows, :].astype(F32)
            gain = gain_ref[pl.ds(y_lo * 8 + f, 1), 0, :]
            tg[u, f, rows, :] = (raw * gain).astype(BF16)
            square = raw * raw
            sq[u, rows, :] += square[:, 0:128] + square[:, 128:256] + square[:, 256:384] + square[:, 384:512]
            return carry

        lax.fori_loop(0, PIECE // 64, body, 0)

    def taken(indices, pieces):
        for index in indices:
            for q in pieces:
                scaled(index, q, core)
                d_copy(index, q, 1 - core).wait_recv()
                scaled(index, q, 1 - core)

    acc[...] = jnp.zeros_like(acc)
    sq[...] = jnp.zeros_like(sq)
    y_arrived(0)
    w_step(0, 2)
    y_far_arrived(0)
    y_arrived(1)
    y_far_arrived(1)
    w_step(0, 3)
    y_arrived(2)
    y_far_arrived(2)
    y_arrived(3)
    y_far_arrived(3)
    x_arrived(0, 0)
    w_step(0, 4)
    x_arrived(0, 1)

    spread = (
        lax.broadcasted_iota(jnp.int32, (TAPS, 2 * TAPS), 0) + lax.broadcasted_iota(jnp.int32, (TAPS, 2 * TAPS), 1)
        == TAPS
    ).astype(F32)
    first = jnp.dot(taps_ref[...], spread, precision=lax.Precision.HIGHEST, preferred_element_type=F32)
    for g in range(16):
        row = jnp.broadcast_to(first[g : g + 1, :], (TAPS, 2 * TAPS))
        matrix = pltpu.roll(row, 0, 1, stride=1, stride_axis=0)
        high = matrix.astype(BF16)
        toep[0, g] = high
        toep[1, g] = (matrix - high.astype(F32)).astype(BF16)

    w_step(0, 5)
    x_arrived(0, 2)
    taken((0, 1), range(PIECES // 2))
    w_step(0, 6)
    x_arrived(0, 3)
    for i in (0, 2, 1, 3, 4, 6, 5, 7, 12, 13):
        o_copy(i).start()
    taken((0, 1), range(PIECES // 2, PIECES))
    w_step(0, 7)
    for h in range(2):
        own_w[2 + h].wait()
        for direction in range(2):
            w_copy(1, direction, h).start()
    for q in range(PIECES):
        x_arrived(1, q)
        taken((2, 3), (q,))
    taken((4, 5), range(PIECES))

    def add_kv(u, low, count, first, chunks):
        rows = pl.ds(low, count)

        def body(j, carry):
            f = (x_far * 2 + first + j) % 8
            lhs0, lhs1 = tg[u, f, rows, 0:256], tg[u, f, rows, 256:512]
            for p in range(2):
                part = jnp.dot(lhs0, wkv[f, 0, p], preferred_element_type=F32)
                part += jnp.dot(lhs1, wkv[f, 1, p], preferred_element_type=F32)
                acc[u, 1 + p, rows, :] += part
            return carry

        lax.fori_loop(0, chunks, body, 0)

    for direction in range(2):
        w_wait(0, direction, 6)
    w_step(1, 2)

    def add_near(i, carry):
        add_kv(i // 2, pl.multiple_of((i % 2) * 256, 256), 256, 2, 6)
        return carry

    lax.fori_loop(0, 4, add_near, 0)
    x_arrived(2, 0)
    x_arrived(2, 1)
    taken((6, 7), (0, 1))
    w_step(1, 3)
    x_arrived(2, 2)
    x_arrived(2, 3)
    taken((6, 7), (2, 3))

    def row_sums(u):
        column = jnp.sum(sq[u], axis=1, keepdims=True)
        return jnp.transpose(jnp.broadcast_to(column, (ROWS, 128)))[0:8, :]

    ss[...] = row_sums(other)
    s_copy = remote(ss, sr, s_send, s_recv, mate)
    s_copy.start()

    def add_q(u, f, low, count):
        rows = pl.ds(low, count)
        part = jnp.dot(tg[u, f, rows, 0:256], wq[f, 0], preferred_element_type=F32)
        part += jnp.dot(tg[u, f, rows, 256:512], wq[f, 1], preferred_element_type=F32)
        return acc[u, 0, rows, :] + part

    def add_q_chunk(f):
        for u in range(2):
            for low in (0, 256):
                acc[u, 0, pl.ds(low, 256), :] = add_q(u, f, low, 256)

    kv_cuts = ((240, 272), (0, 240))

    def c_kv(i):
        rows = pl.ds(*kv_cuts[i])
        planes = pl.ds(1, 2)
        return remote(cs.at[planes, rows, :], cr.at[planes, rows, :], c_send.at[i], c_recv.at[i], mate)

    def c_q(r):
        rows = pl.ds(CUTS[r], CUTS[r + 1] - CUTS[r])
        return remote(cs.at[0, rows, :], cr.at[0, rows, :], c_send.at[2 + r], c_recv.at[2 + r], mate)

    def give_kv(i):
        add_kv(other, *kv_cuts[i], 0, 2)
        rows = pl.ds(*kv_cuts[i])
        for p in (1, 2):
            cs[p, rows, :] = acc[other, p, rows, :].astype(BF16)
        c_kv(i).start()

    def finish(p, low, count):
        rows = pl.ds(low, count)
        factor = sq[0, rows, :]
        factor = jnp.concatenate([factor, factor], axis=1)
        value = acc[y_lo, p, rows, :] + cr[p, rows, :].astype(F32)
        pj[p, pl.ds(16 + low, count), :] = (value * factor).astype(BF16)

    def filtered(p, low, n):
        extended = pj[p, pl.ds(low, n + 16), :].astype(F32)
        taps = [short_ref[k, pl.ds(p, 1), :] for k in range(3)]
        return taps[0] * extended[16 : n + 16] + taps[1] * extended[15 : n + 15] + taps[2] * extended[14 : n + 14]

    def make_product(r):
        pe[pl.ds(128 + r * 128, 128), :] = (filtered(1, r * 128, 128) * filtered(2, r * 128, 128)).astype(BF16)

    kv_planes = pl.ds(1, 2)
    halo_kv = [
        remote(pe.at[pl.ds(512, 128), :], pe.at[pl.ds(0, 128), :], h_send.at[0], h_recv.at[0], after),
        remote(pj.at[kv_planes, pl.ds(512, 16), :], pj.at[kv_planes, pl.ds(0, 16), :], h_send.at[1], h_recv.at[1], after),
    ]
    halo_q = remote(pj.at[0, pl.ds(512, 16), :], pj.at[0, pl.ds(0, 16), :], h_send.at[2], h_recv.at[2], after)
    has_after, has_before = s < 15, s > 0

    group_of_lane = lax.broadcasted_iota(jnp.int32, (128, CH), 1) // GROUP

    def make_mixing(r):
        window = pe[pl.ds(r * 128, 256), :]

        def body(g, mixed):
            part = jnp.dot(toep[0, g], window, preferred_element_type=F32)
            part += jnp.dot(toep[1, g], window, preferred_element_type=F32)
            return jnp.where(group_of_lane == g, part, mixed)

        mixed = lax.fori_loop(0, 16, body, jnp.zeros((128, CH), F32), unroll=4)
        product = pe[pl.ds(128 + r * 128, 128), :].astype(F32)
        mix[pl.ds(r * 128, 128), :] = skip_ref[...] * product + mixed

    give_kv(0)
    w_step(1, 4)
    give_kv(1)
    add_kv(y_lo, 240, 272, 0, 2)
    w_step(1, 5)
    add_kv(y_lo, 0, 240, 0, 2)
    w_step(1, 6)
    s_copy.wait()
    total = row_sums(y_lo) + sr[...]
    factor = lax.rsqrt(total * (1.0 / 8192.0) + EPSILON)
    sq[0] = jnp.transpose(jnp.broadcast_to(factor[0:1, :], (128, ROWS)))

    @pl.when(s == 0)
    def _():
        pe[pl.ds(0, 128), :] = jnp.zeros((128, CH), BF16)
        pj[:, pl.ds(0, 16), :] = jnp.zeros((3, 16, CH), BF16)

    c_kv(0).wait_recv()
    for p in (1, 2):
        finish(p, *kv_cuts[0])
    make_product(3)

    @pl.when(has_after)
    def _():
        for cp in halo_kv:
            cp.start()

    make_product(2)
    w_step(1, 7)
    add_q_chunk(z)
    for distance in (1, 2, 3):
        add_q_chunk((z + distance) % 8)
        add_q_chunk((z + 8 - distance) % 8)
    o_keep.wait()
    keep_x.wait()

    for direction in range(2):
        w_wait(1, direction, 6)
    f_last = (z + 4) % 8
    order = range(CHUNKS - 1, -1, -1)
    for r in order:
        low, count = CUTS[r], CUTS[r + 1] - CUTS[r]
        cs[0, pl.ds(low, count), :] = add_q(other, f_last, low, count).astype(BF16)
        c_q(r).start()
    for i in SHARED:
        o_wait(i)
        m_copy(i).start()
    for low in (256, 0):
        acc[y_lo, 0, pl.ds(low, 256), :] = add_q(y_lo, f_last, low, 256)

    make_mixing(3)
    c_kv(1).wait_recv()
    for p in (1, 2):
        finish(p, *kv_cuts[1])
    make_product(1)
    make_mixing(2)

    held = [(y_hi, x), (1 - y_hi, x)]
    for y_hi_ in (y_hi, 1 - y_hi):
        held += [(y_hi_, x_left), (y_hi_, x_right)]
    held += [(y_hi, x_far), (1 - y_hi, x_far)]

    def part_of(index, core_, r):
        y_hi_, x_ = held[index]
        return gate.at[y_hi_ * 8 + x_ * 2 + core_, pl.ds(r * CHUNK, CHUNK), :]

    def t_copy(index, r):
        place = part_of(index, core, r)
        return remote(place, place, t_send.at[r, index], t_recv.at[r, index], twin)

    def v_copy(r):
        place = part_of(0, core, r)
        return remote(place, place, v_send.at[r], v_recv.at[r], opposite)

    def a_copy(direction, k, r):
        index = k if k < 2 else 2 if direction == 0 else 5
        place = part_of(index, core, r)
        return remote(
            place, place, a_send.at[r, direction, k], a_recv.at[r, direction, k], right if direction == 0 else left
        )

    def a_arrived(k, r):
        for direction in range(2):
            index = 2 + 2 * k + direction
            place = part_of(index, core, r)
            remote(place, place, a_send.at[r, direction, k], a_recv.at[r, direction, k], right).wait_recv()
            if k == direction:
                a_copy(direction, 2, r).start()
            t_copy(index, r).start()

    def v_arrived(r):
        place = part_of(1, core, r)
        remote(place, place, v_send.at[r], v_recv.at[r], opposite).wait_recv()
        for direction in range(2):
            a_copy(direction, 1, r).start()
        t_copy(1, r).start()

    def make_gating(r):
        rows = pl.ds(r * CHUNK, CHUNK)
        gate[c, rows, :] = (filtered(0, r * CHUNK, CHUNK) * mix[rows, :]).astype(BF16)
        v_copy(r).start()
        for direction in range(2):
            a_copy(direction, 0, r).start()
        t_copy(0, r).start()

    def arrive_q(r):
        c_q(r).wait_recv()
        finish(0, CUTS[r], CUTS[r + 1] - CUTS[r])

    def write(r):
        for index in range(8):
            place = part_of(index, 1 - core, r)
            remote(place, place, t_send.at[r, index], t_recv.at[r, index], twin).wait_recv()

        def body(half, carry):
            rows = pl.ds(r * CHUNK, CHUNK)
            columns = pl.ds(pl.multiple_of(half * 256, 256), 256)
            total = xres[rows, columns].astype(F32)
            for i in range(16):
                total += jnp.dot(gate[i, rows, :], wo[i, :, columns], preferred_element_type=F32)
            out_ref[rows, columns] = total.astype(BF16)
            return carry

        lax.fori_loop(0, 2, body, 0)

    for r in order:
        arrive_q(r)
        if r == CHUNKS - 1:

            @pl.when(has_after)
            def _():
                halo_q.start()

        if r == 0:

            @pl.when(has_before)
            def _():
                halo_q.wait_recv()

        make_gating(r)
        if r == CHUNKS - 1:

            @pl.when(has_before)
            def _():
                for cp in halo_kv:
                    cp.wait_recv()

            make_product(0)
            make_mixing(1)
            make_mixing(0)
    for r in order:
        v_arrived(r)
        a_arrived(0, r)
    for i in range(15):
        if i not in SHARED:
            o_wait(i)
    for i in SHARED:
        m_wait(i)
    for r in order:
        a_arrived(1, r)
    for r in order:
        a_arrived(2, r)
        write(r)

    for direction in range(2):
        for k in range(7):
            for phase in range(2):
                w_copy(phase, direction, k).wait_send()
        for k in range(3):
            for q in range(PIECES):
                x_copy(direction, k, q).wait_send()
    @pl.when(jnp.logical_not(is_home))
    def _():
        for d in range(2):
            for q in range(PIECES):
                y_copy(d, q).wait_send()

    @pl.when(is_home)
    def _():
        for q in range(PIECES):
            f_copy(q).wait_send()
            f_pass(q).wait_send()

    for index in range(8):
        for q in range(PIECES):
            d_copy(index, q, core).wait_send()
    for i in range(2):
        c_kv(i).wait_send()
    for i in range(15):
        o_copy(i).wait_send()
    for i in SHARED:
        m_copy(i).wait_send()
    for r in range(CHUNKS):
        c_q(r).wait_send()
        v_copy(r).wait_send()
        for index in range(8):
            t_copy(index, r).wait_send()
        for direction in range(2):
            for k in range(3):
                a_copy(direction, k, r).wait_send()

    @pl.when(has_after)
    def _():
        for cp in halo_kv + [halo_q]:
            cp.wait_send()


def block_call(tokens, gain, w_planes, short_taps, taps, skip, w_out):
    dma = pltpu.SemaphoreType.DMA
    vmem = pl.BlockSpec(memory_space=pltpu.VMEM)
    far = pl.BlockSpec(memory_space=pl.ANY)
    return pl.pallas_call(
        block_kernel,
        out_shape=jax.ShapeDtypeStruct((ROWS, WIDE), BF16),
        in_specs=[far, vmem, far, vmem, vmem, vmem, far],
        out_specs=vmem,
        scratch_shapes=[
            pltpu.VMEM((2, 8, ROWS, WIDE), BF16),
            pltpu.VMEM((2, 8, ROWS, WIDE), BF16),
            pltpu.VMEM((8, 2, 2, 256, CH), BF16),
            pltpu.VMEM((8, 2, 256, CH), BF16),
            pltpu.VMEM((ROWS, WIDE), BF16),
            pltpu.VMEM((2, 3, ROWS, CH), F32),
            pltpu.VMEM((3, ROWS, CH), BF16),
            pltpu.VMEM((3, ROWS, CH), BF16),
            pltpu.VMEM((2, ROWS, 128), F32),
            pltpu.VMEM((8, ROWS), F32),
            pltpu.VMEM((8, ROWS), F32),
            pltpu.VMEM((16, CH, WIDE), BF16),
            pltpu.VMEM((2, 16, TAPS, 2 * TAPS), BF16),
            pltpu.VMEM((3, 16 + ROWS, CH), BF16),
            pltpu.VMEM((128 + ROWS, CH), BF16),
            pltpu.VMEM((ROWS, CH), F32),
            pltpu.VMEM((16, ROWS, CH), BF16),
            pltpu.VMEM((ROWS, WIDE), BF16),
            dma((10,)),
            dma((2, 2, 7)), dma((2, 2, 7)),
            dma((2, PIECES)), dma((2, PIECES)),
            dma((PIECES,)), dma((PIECES,)),
            dma((2, 3, PIECES)), dma((2, 3, PIECES)),
            dma((8, PIECES)), dma((8, PIECES)),
            dma((6,)), dma((6,)),
            dma, dma,
            dma((15,)), dma((16,)),
            dma((12,)), dma((12,)),
            dma((3,)), dma((3,)),
            dma((CHUNKS,)), dma((CHUNKS,)),
            dma((CHUNKS, 2, 3)), dma((CHUNKS, 2, 3)),
            dma((CHUNKS, 8)), dma((CHUNKS, 8)),
        ],
        compiler_params=pltpu.CompilerParams(
            collective_id=0, has_side_effects=True, vmem_limit_bytes=58 * 1024 * 1024
        ),
        name="block",
    )(tokens, gain, w_planes, short_taps, taps, skip, w_out)


def per_device(tokens, norm_gain, w_in, short_taps, medium_taps, skip_gain, w_out):
    return block_call(
        tokens,
        norm_gain.reshape(16, 1, WIDE),
        jnp.transpose(w_in, (1, 0, 2)),
        short_taps,
        jnp.transpose(medium_taps),
        skip_gain.reshape(1, CH),
        w_out,
    )


def solution(mesh):
    in_specs = (
        P("seq", "chan"),
        P(),
        P("seq", None, "chan"),
        P(None, None, "chan"),
        P(None, "chan"),
        P("chan"),
        P("chan", None),
    )
    out_specs = P("seq", "chan")
    return jax.shard_map(
        per_device, mesh=mesh, in_specs=in_specs, out_specs=out_specs, check_vma=False
    )
```

```python
import jax
import jax.numpy as jnp
from jax import lax
from jax.experimental import pallas as pl
from jax.experimental.pallas import tpu as pltpu
from jax.sharding import PartitionSpec as P

TAPS = 128
GROUP = 16
EPSILON = 1e-06
MESH = pl.DeviceIdType.MESH
ROWS = 512
WIDE = 512
CH = 256
F32 = jnp.float32
BF16 = jnp.bfloat16
PIECES = 4
PIECE = ROWS // PIECES
CHUNKS = 2
CHUNK = ROWS // CHUNKS
CUTS = [0] + [r * CHUNK - 16 for r in range(1, CHUNKS)] + [ROWS]


def block_kernel(
    x_hbm, gain_ref, w_hbm, short_ref, taps_ref, skip_ref, wo_hbm, out_ref,
    tok, tg, wkv, wq, stage, acc, cs, cr, sq, ss, sr, wo, toep, pj, pe, mix, gate, xres,
    loc, w_send, w_recv, y_send, y_recv, f_send, f_recv, x_send, x_recv, d_send, d_recv, c_send, c_recv, s_send, s_recv,
    o_send, o_recv, m_send, m_recv, h_send, h_recv, v_send, v_recv, a_send, a_recv, t_send, t_recv,
):
    s = lax.axis_index("seq")
    c = lax.axis_index("chan")
    y_lo, z = s // 8, s % 8
    y_hi, x, core = c // 8, (c // 2) % 4, c % 2
    f_own = x * 2 + core
    x_right, x_left, x_far = (x + 1) % 4, (x + 3) % 4, (x + 2) % 4
    other = 1 - y_lo

    def at(y_hi_=y_hi, x_=x, core_=core, y_lo_=y_lo, z_=z):
        return (y_lo_ * 8 + z_, y_hi_ * 8 + x_ * 2 + core_)

    right, left = at(x_=x_right), at(x_=x_left)
    up, down = at(z_=(z + 1) % 8), at(z_=(z + 7) % 8)
    twin = at(core_=1 - core)
    mate = at(y_lo_=other)
    opposite = at(y_hi_=1 - y_hi)
    diagonal = at(y_hi_=1 - y_hi, y_lo_=other)
    after, before = ((s + 1) % 16, c), ((s + 15) % 16, c)

    def remote(src, dst, send, recv, device):
        return pltpu.make_async_remote_copy(
            src_ref=src, dst_ref=dst, send_sem=send, recv_sem=recv, device_id=device, device_id_type=MESH
        )

    own_w = []
    for h in range(2):
        rows = pl.ds(h * 256, 256)
        own_w.append(pltpu.make_async_copy(w_hbm.at[pl.ds(1, 2), rows, :], wkv.at[z, h], loc.at[h]))
    for h in range(2):
        rows = pl.ds(h * 256, 256)
        own_w.append(pltpu.make_async_copy(w_hbm.at[0, rows, :], wq.at[z, h], loc.at[2 + h]))
    for cp in own_w:
        cp.start()

    barrier = pltpu.get_barrier_semaphore()
    def w_out_peers(y_hi_, y_lo_, xs):
        return [at(y_hi_=y_hi_, y_lo_=y_lo_, x_=x_, core_=k) for x_ in xs for k in range(2)]

    o_peers = (
        w_out_peers(y_hi, y_lo, (x_right, x_left))
        + w_out_peers(1 - y_hi, other, (x_right, x_left))
        + w_out_peers(y_hi, y_lo, (x_far,))
        + w_out_peers(1 - y_hi, other, (x_far, x))
        + [twin]
    )
    peers = o_peers + [up, down, mate, opposite, after, before]
    for peer in peers:
        pl.semaphore_signal(barrier, inc=1, device_id=peer, device_id_type=MESH)
    pl.semaphore_wait(barrier, len(peers))

    def w_slot(phase, direction, distance, half):
        source = (z + 8 - distance) % 8 if direction == 0 else (z + distance) % 8
        return (wkv, wq)[phase].at[source, half]

    def recv_place(direction, k):
        if k == 6:
            return 4, direction
        return k // 2 + 1, k % 2

    def send_place(direction, k):
        if k < 2:
            return 0, k
        if k == 6:
            return 3, direction
        return (k - 2) // 2 + 1, (k - 2) % 2

    def w_copy(phase, direction, k):
        slot = w_slot(phase, direction, *send_place(direction, k))
        return remote(
            slot, slot, w_send.at[phase, direction, k], w_recv.at[phase, direction, k], up if direction == 0 else down
        )

    def w_wait(phase, direction, k):
        slot = w_slot(phase, direction, *recv_place(direction, k))
        remote(slot, slot, w_send.at[phase, direction, k], w_recv.at[phase, direction, k], up).wait_recv()

    def w_step(phase, k):
        for direction in range(2):
            w_wait(phase, direction, k - 2)
            if k < 6:
                w_copy(phase, direction, k).start()
            elif k - 6 == direction:
                w_copy(phase, direction, 6).start()

    for h in range(2):
        own_w[h].wait()
        for direction in range(2):
            w_copy(0, direction, h).start()

    is_home = y_hi == y_lo

    def piece(q):
        return pl.ds(q * PIECE, PIECE)

    def y_copy(d, q):
        return remote(
            x_hbm.at[piece(q), :], tok.at[y_lo, f_own, piece(q), :],
            y_send.at[d, q], y_recv.at[y_lo, q], at(y_lo_=y_hi, y_hi_=d),
        )

    def y_keep(q):
        return pltpu.make_async_copy(x_hbm.at[piece(q), :], tok.at[y_lo, f_own, piece(q), :], loc.at[5 + q])

    SHARED = (8, 9, 10, 11)
    odd = z % 2
    buddy = at(z_=z + 1 - 2 * odd)

    def o_rows(i, half):
        return pl.ds(pl.multiple_of(half * 128, 128), 128) if i in SHARED else pl.ds(0, 256)

    def o_copy(i):
        device = o_peers[i]
        rows = o_rows(i, odd)
        there = wo_hbm.at[rows, pl.ds(pl.multiple_of(device[1] * WIDE, WIDE), WIDE)]
        return remote(there, wo.at[c, rows, :], o_send.at[i], o_recv.at[c], device)

    def o_wait(i):
        source = o_peers[i][1]
        slot = wo.at[source, o_rows(i, odd), :]
        remote(slot, slot, o_send.at[i], o_recv.at[source], twin).wait_recv()

    def m_copy(i):
        slot = wo.at[o_peers[i][1], o_rows(i, odd), :]
        return remote(slot, slot, m_send.at[i], m_recv.at[i], buddy)

    def m_wait(i):
        slot = wo.at[o_peers[i][1], o_rows(i, 1 - odd), :]
        remote(slot, slot, m_send.at[i], m_recv.at[i], buddy).wait_recv()

    o_keep = pltpu.make_async_copy(wo_hbm.at[:, pl.ds(pl.multiple_of(c * WIDE, WIDE), WIDE)], wo.at[c], loc.at[9])

    def f_copy(q):
        return remote(x_hbm.at[piece(q), :], stage.at[piece(q), :], f_send.at[q], f_recv.at[q], diagonal)

    def f_pass(q):
        return remote(
            stage.at[piece(q), :], tok.at[other, f_own, piece(q), :], y_send.at[1 - y_hi, q], y_recv.at[other, q], mate
        )

    for q in range(PIECES):
        for d in range(2):
            stays = jnp.logical_and(is_home, y_hi == d)

            @pl.when(jnp.logical_not(is_home))
            def _():
                y_copy(d, q).start()

            @pl.when(stays)
            def _():
                y_keep(q).start()
                f_copy(q).start()

    for i in (8, 9, 10, 11):
        o_copy(i).start()
    o_copy(14).start()
    o_keep.start()
    keep_x = pltpu.make_async_copy(x_hbm, xres, loc.at[4])
    keep_x.start()

    def x_place(direction, k):
        u = direction if k != 1 else 1 - direction
        return u, (x_far if k == 2 else x_left if direction == 0 else x_right)

    def x_copy(direction, k, q):
        if k < 2:
            slot = tok.at[direction if k == 0 else 1 - direction, f_own, piece(q), :]
        else:
            slot = tok.at[direction, (x_left if direction == 0 else x_right) * 2 + core, piece(q), :]
        return remote(
            slot, slot, x_send.at[direction, k, q], x_recv.at[direction, k, q], right if direction == 0 else left
        )

    def x_wait(direction, k, q):
        u, source = x_place(direction, k)
        slot = tok.at[u, source * 2 + core, piece(q), :]
        remote(slot, slot, x_send.at[direction, k, q], x_recv.at[direction, k, q], right).wait_recv()

    places = [(0, x), (1, x)] + [x_place(direction, k) for k in range(3) for direction in range(2)]

    def d_copy(index, q, core_):
        u, source = places[index]
        slot = tok.at[u, source * 2 + core_, piece(q), :]
        return remote(slot, slot, d_send.at[index, q], d_recv.at[index, q], twin)

    def send_own(u, q):
        for direction in range(2):
            k = 1 - u if direction else u
            slot = tok.at[u, f_own, piece(q), :]
            remote(
                slot, slot, x_send.at[direction, k, q], x_recv.at[direction, k, q], right if direction == 0 else left
            ).start()
        slot = tok.at[u, f_own, piece(q), :]
        remote(slot, slot, d_send.at[u, q], d_recv.at[u, q], twin).start()

    def y_arrived(q):
        slot = tok.at[other, f_own, piece(q), :]
        remote(slot, slot, y_send.at[0, q], y_recv.at[other, q], right).wait_recv()
        send_own(other, q)

    def y_far_arrived(q):
        slot = tok.at[y_lo, f_own, piece(q), :]

        @pl.when(is_home)
        def _():
            remote(stage.at[piece(q), :], stage.at[piece(q), :], f_send.at[q], f_recv.at[q], right).wait_recv()
            f_pass(q).start()
            y_keep(q).wait()

        @pl.when(jnp.logical_not(is_home))
        def _():
            remote(slot, slot, y_send.at[0, q], y_recv.at[y_lo, q], right).wait_recv()

        send_own(y_lo, q)

    def x_arrived(k, q):
        for direction in range(2):
            x_wait(direction, k, q)
            if k == 0:
                x_copy(direction, 2, q).start()
            d_copy(2 + 2 * k + direction, q, core).start()

    def scaled(index, q, core_):
        u, source = places[index]
        f = source * 2 + core_

        def body(i, carry):
            rows = pl.ds(pl.multiple_of(q * PIECE + i * 64, 64), 64)
            raw = tok[u, f, rows, :].astype(F32)
            gain = gain_ref[pl.ds(y_lo * 8 + f, 1), 0, :]
            tg[u, f, rows, :] = (raw * gain).astype(BF16)
            square = raw * raw
            sq[u, rows, :] += square[:, 0:128] + square[:, 128:256] + square[:, 256:384] + square[:, 384:512]
            return carry

        lax.fori_loop(0, PIECE // 64, body, 0)

    def taken(indices, pieces):
        for index in indices:
            for q in pieces:
                scaled(index, q, core)
                d_copy(index, q, 1 - core).wait_recv()
                scaled(index, q, 1 - core)

    acc[...] = jnp.zeros_like(acc)
    sq[...] = jnp.zeros_like(sq)
    y_arrived(0)
    w_step(0, 2)
    y_far_arrived(0)
    y_arrived(1)
    y_far_arrived(1)
    w_step(0, 3)
    y_arrived(2)
    y_far_arrived(2)
    y_arrived(3)
    y_far_arrived(3)
    x_arrived(0, 0)
    w_step(0, 4)
    x_arrived(0, 1)

    spread = (
        lax.broadcasted_iota(jnp.int32, (TAPS, 2 * TAPS), 0) + lax.broadcasted_iota(jnp.int32, (TAPS, 2 * TAPS), 1)
        == TAPS
    ).astype(F32)
    first = jnp.dot(taps_ref[...], spread, precision=lax.Precision.HIGHEST, preferred_element_type=F32)
    for g in range(16):
        row = jnp.broadcast_to(first[g : g + 1, :], (TAPS, 2 * TAPS))
        matrix = pltpu.roll(row, 0, 1, stride=1, stride_axis=0)
        high = matrix.astype(BF16)
        toep[0, g] = high
        toep[1, g] = (matrix - high.astype(F32)).astype(BF16)

    w_step(0, 5)
    x_arrived(0, 2)
    taken((0, 1), range(PIECES // 2))
    w_step(0, 6)
    x_arrived(0, 3)
    for i in (0, 2, 1, 3, 4, 6, 5, 7, 12, 13):
        o_copy(i).start()
    taken((0, 1), range(PIECES // 2, PIECES))
    w_step(0, 7)
    for h in range(2):
        own_w[2 + h].wait()
        for direction in range(2):
            w_copy(1, direction, h).start()
    for q in range(PIECES):
        x_arrived(1, q)
        taken((2, 3), (q,))
    taken((4, 5), range(PIECES))

    def add_kv(u, low, count, first, chunks):
        rows = pl.ds(low, count)

        def body(j, carry):
            f = (x_far * 2 + first + j) % 8
            lhs0, lhs1 = tg[u, f, rows, 0:256], tg[u, f, rows, 256:512]
            for p in range(2):
                part = jnp.dot(lhs0, wkv[f, 0, p], preferred_element_type=F32)
                part += jnp.dot(lhs1, wkv[f, 1, p], preferred_element_type=F32)
                acc[u, 1 + p, rows, :] += part
            return carry

        lax.fori_loop(0, chunks, body, 0)

    for direction in range(2):
        w_wait(0, direction, 6)
    w_step(1, 2)

    def add_near(i, carry):
        add_kv(i // 2, pl.multiple_of((i % 2) * 256, 256), 256, 2, 6)
        return carry

    lax.fori_loop(0, 4, add_near, 0)
    x_arrived(2, 0)
    x_arrived(2, 1)
    taken((6, 7), (0, 1))
    w_step(1, 3)
    x_arrived(2, 2)
    x_arrived(2, 3)
    taken((6, 7), (2, 3))

    def row_sums(u):
        column = jnp.sum(sq[u], axis=1, keepdims=True)
        return jnp.transpose(jnp.broadcast_to(column, (ROWS, 128)))[0:8, :]

    ss[...] = row_sums(other)
    s_copy = remote(ss, sr, s_send, s_recv, mate)
    s_copy.start()

    def add_q(u, f, low, count):
        rows = pl.ds(low, count)
        part = jnp.dot(tg[u, f, rows, 0:256], wq[f, 0], preferred_element_type=F32)
        part += jnp.dot(tg[u, f, rows, 256:512], wq[f, 1], preferred_element_type=F32)
        return acc[u, 0, rows, :] + part

    def add_q_chunk(f):
        for u in range(2):
            for low in (0, 256):
                acc[u, 0, pl.ds(low, 256), :] = add_q(u, f, low, 256)

    kv_cuts = ((240, 272), (0, 240))

    def c_kv(i):
        rows = pl.ds(*kv_cuts[i])
        planes = pl.ds(1, 2)
        return remote(cs.at[planes, rows, :], cr.at[planes, rows, :], c_send.at[i], c_recv.at[i], mate)

    def c_q(r):
        rows = pl.ds(CUTS[r], CUTS[r + 1] - CUTS[r])
        return remote(cs.at[0, rows, :], cr.at[0, rows, :], c_send.at[2 + r], c_recv.at[2 + r], mate)

    def give_kv(i):
        add_kv(other, *kv_cuts[i], 0, 2)
        rows = pl.ds(*kv_cuts[i])
        for p in (1, 2):
            cs[p, rows, :] = acc[other, p, rows, :].astype(BF16)
        c_kv(i).start()

    def finish(p, low, count):
        rows = pl.ds(low, count)
        factor = sq[0, rows, :]
        factor = jnp.concatenate([factor, factor], axis=1)
        value = acc[y_lo, p, rows, :] + cr[p, rows, :].astype(F32)
        pj[p, pl.ds(16 + low, count), :] = (value * factor).astype(BF16)

    def filtered(p, low, n):
        extended = pj[p, pl.ds(low, n + 16), :].astype(F32)
        taps = [short_ref[k, pl.ds(p, 1), :] for k in range(3)]
        return taps[0] * extended[16 : n + 16] + taps[1] * extended[15 : n + 15] + taps[2] * extended[14 : n + 14]

    def make_product(r):
        pe[pl.ds(128 + r * 128, 128), :] = (filtered(1, r * 128, 128) * filtered(2, r * 128, 128)).astype(BF16)

    kv_planes = pl.ds(1, 2)
    halo_kv = [
        remote(pe.at[pl.ds(512, 128), :], pe.at[pl.ds(0, 128), :], h_send.at[0], h_recv.at[0], after),
        remote(pj.at[kv_planes, pl.ds(512, 16), :], pj.at[kv_planes, pl.ds(0, 16), :], h_send.at[1], h_recv.at[1], after),
    ]
    halo_q = remote(pj.at[0, pl.ds(512, 16), :], pj.at[0, pl.ds(0, 16), :], h_send.at[2], h_recv.at[2], after)
    has_after, has_before = s < 15, s > 0

    group_of_lane = lax.broadcasted_iota(jnp.int32, (128, CH), 1) // GROUP

    def make_mixing(r):
        window = pe[pl.ds(r * 128, 256), :]

        def body(g, mixed):
            part = jnp.dot(toep[0, g], window, preferred_element_type=F32)
            part += jnp.dot(toep[1, g], window, preferred_element_type=F32)
            return jnp.where(group_of_lane == g, part, mixed)

        mixed = lax.fori_loop(0, 16, body, jnp.zeros((128, CH), F32), unroll=4)
        product = pe[pl.ds(128 + r * 128, 128), :].astype(F32)
        mix[pl.ds(r * 128, 128), :] = skip_ref[...] * product + mixed

    give_kv(0)
    w_step(1, 4)
    give_kv(1)
    add_kv(y_lo, 240, 272, 0, 2)
    w_step(1, 5)
    add_kv(y_lo, 0, 240, 0, 2)
    w_step(1, 6)
    s_copy.wait()
    total = row_sums(y_lo) + sr[...]
    factor = lax.rsqrt(total * (1.0 / 8192.0) + EPSILON)
    sq[0] = jnp.transpose(jnp.broadcast_to(factor[0:1, :], (128, ROWS)))

    @pl.when(s == 0)
    def _():
        pe[pl.ds(0, 128), :] = jnp.zeros((128, CH), BF16)
        pj[:, pl.ds(0, 16), :] = jnp.zeros((3, 16, CH), BF16)

    c_kv(0).wait_recv()
    for p in (1, 2):
        finish(p, *kv_cuts[0])
    make_product(3)

    @pl.when(has_after)
    def _():
        for cp in halo_kv:
            cp.start()

    make_product(2)
    w_step(1, 7)
    add_q_chunk(z)
    for distance in (1, 2, 3):
        add_q_chunk((z + distance) % 8)
        add_q_chunk((z + 8 - distance) % 8)
    o_keep.wait()
    keep_x.wait()

    for direction in range(2):
        w_wait(1, direction, 6)
    f_last = (z + 4) % 8
    order = range(CHUNKS - 1, -1, -1)
    for r in order:
        low, count = CUTS[r], CUTS[r + 1] - CUTS[r]
        cs[0, pl.ds(low, count), :] = add_q(other, f_last, low, count).astype(BF16)
        c_q(r).start()
    for i in SHARED:
        o_wait(i)
        m_copy(i).start()
    for low in (256, 0):
        acc[y_lo, 0, pl.ds(low, 256), :] = add_q(y_lo, f_last, low, 256)

    make_mixing(3)
    c_kv(1).wait_recv()
    for p in (1, 2):
        finish(p, *kv_cuts[1])
    make_product(1)
    make_mixing(2)

    held = [(y_hi, x), (1 - y_hi, x)]
    for y_hi_ in (y_hi, 1 - y_hi):
        held += [(y_hi_, x_left), (y_hi_, x_right)]
    held += [(y_hi, x_far), (1 - y_hi, x_far)]

    def part_of(index, core_, r):
        y_hi_, x_ = held[index]
        return gate.at[y_hi_ * 8 + x_ * 2 + core_, pl.ds(r * CHUNK, CHUNK), :]

    def t_copy(index, r):
        place = part_of(index, core, r)
        return remote(place, place, t_send.at[r, index], t_recv.at[r, index], twin)

    def v_copy(r):
        place = part_of(0, core, r)
        return remote(place, place, v_send.at[r], v_recv.at[r], opposite)

    def a_copy(direction, k, r):
        index = k if k < 2 else 2 if direction == 0 else 5
        place = part_of(index, core, r)
        return remote(
            place, place, a_send.at[r, direction, k], a_recv.at[r, direction, k], right if direction == 0 else left
        )

    def a_arrived(k, r):
        for direction in range(2):
            index = 2 + 2 * k + direction
            place = part_of(index, core, r)
            remote(place, place, a_send.at[r, direction, k], a_recv.at[r, direction, k], right).wait_recv()
            if k == direction:
                a_copy(direction, 2, r).start()
            t_copy(index, r).start()

    def v_arrived(r):
        place = part_of(1, core, r)
        remote(place, place, v_send.at[r], v_recv.at[r], opposite).wait_recv()
        for direction in range(2):
            a_copy(direction, 1, r).start()
        t_copy(1, r).start()

    def make_gating(r):
        rows = pl.ds(r * CHUNK, CHUNK)
        gate[c, rows, :] = (filtered(0, r * CHUNK, CHUNK) * mix[rows, :]).astype(BF16)
        v_copy(r).start()
        for direction in range(2):
            a_copy(direction, 0, r).start()
        t_copy(0, r).start()

    def arrive_q(r):
        c_q(r).wait_recv()
        finish(0, CUTS[r], CUTS[r + 1] - CUTS[r])

    def write(r):
        for index in range(8):
            place = part_of(index, 1 - core, r)
            remote(place, place, t_send.at[r, index], t_recv.at[r, index], twin).wait_recv()

        def body(half, carry):
            rows = pl.ds(r * CHUNK, CHUNK)
            columns = pl.ds(pl.multiple_of(half * 256, 256), 256)
            total = xres[rows, columns].astype(F32)
            for i in range(16):
                total += jnp.dot(gate[i, rows, :], wo[i, :, columns], preferred_element_type=F32)
            out_ref[rows, columns] = total.astype(BF16)
            return carry

        lax.fori_loop(0, 2, body, 0)

    for r in order:
        arrive_q(r)
        if r == CHUNKS - 1:

            @pl.when(has_after)
            def _():
                halo_q.start()

        if r == 0:

            @pl.when(has_before)
            def _():
                halo_q.wait_recv()

        make_gating(r)
        if r == CHUNKS - 1:

            @pl.when(has_before)
            def _():
                for cp in halo_kv:
                    cp.wait_recv()

            make_product(0)
            make_mixing(1)
            make_mixing(0)
    for r in order:
        v_arrived(r)
        a_arrived(0, r)
    for r in order:
        a_arrived(1, r)
    for i in range(15):
        if i not in SHARED:
            o_wait(i)
    for i in SHARED:
        m_wait(i)
    for r in order:
        a_arrived(2, r)
        write(r)

    for direction in range(2):
        for k in range(7):
            for phase in range(2):
                w_copy(phase, direction, k).wait_send()
        for k in range(3):
            for q in range(PIECES):
                x_copy(direction, k, q).wait_send()
    @pl.when(jnp.logical_not(is_home))
    def _():
        for d in range(2):
            for q in range(PIECES):
                y_copy(d, q).wait_send()

    @pl.when(is_home)
    def _():
        for q in range(PIECES):
            f_copy(q).wait_send()
            f_pass(q).wait_send()

    for index in range(8):
        for q in range(PIECES):
            d_copy(index, q, core).wait_send()
    for i in range(2):
        c_kv(i).wait_send()
    for i in range(15):
        o_copy(i).wait_send()
    for i in SHARED:
        m_copy(i).wait_send()
    for r in range(CHUNKS):
        c_q(r).wait_send()
        v_copy(r).wait_send()
        for index in range(8):
            t_copy(index, r).wait_send()
        for direction in range(2):
            for k in range(3):
                a_copy(direction, k, r).wait_send()

    @pl.when(has_after)
    def _():
        for cp in halo_kv + [halo_q]:
            cp.wait_send()


def block_call(tokens, gain, w_planes, short_taps, taps, skip, w_out):
    dma = pltpu.SemaphoreType.DMA
    vmem = pl.BlockSpec(memory_space=pltpu.VMEM)
    far = pl.BlockSpec(memory_space=pl.ANY)
    return pl.pallas_call(
        block_kernel,
        out_shape=jax.ShapeDtypeStruct((ROWS, WIDE), BF16),
        in_specs=[far, vmem, far, vmem, vmem, vmem, far],
        out_specs=vmem,
        scratch_shapes=[
            pltpu.VMEM((2, 8, ROWS, WIDE), BF16),
            pltpu.VMEM((2, 8, ROWS, WIDE), BF16),
            pltpu.VMEM((8, 2, 2, 256, CH), BF16),
            pltpu.VMEM((8, 2, 256, CH), BF16),
            pltpu.VMEM((ROWS, WIDE), BF16),
            pltpu.VMEM((2, 3, ROWS, CH), F32),
            pltpu.VMEM((3, ROWS, CH), BF16),
            pltpu.VMEM((3, ROWS, CH), BF16),
            pltpu.VMEM((2, ROWS, 128), F32),
            pltpu.VMEM((8, ROWS), F32),
            pltpu.VMEM((8, ROWS), F32),
            pltpu.VMEM((16, CH, WIDE), BF16),
            pltpu.VMEM((2, 16, TAPS, 2 * TAPS), BF16),
            pltpu.VMEM((3, 16 + ROWS, CH), BF16),
            pltpu.VMEM((128 + ROWS, CH), BF16),
            pltpu.VMEM((ROWS, CH), F32),
            pltpu.VMEM((16, ROWS, CH), BF16),
            pltpu.VMEM((ROWS, WIDE), BF16),
            dma((10,)),
            dma((2, 2, 7)), dma((2, 2, 7)),
            dma((2, PIECES)), dma((2, PIECES)),
            dma((PIECES,)), dma((PIECES,)),
            dma((2, 3, PIECES)), dma((2, 3, PIECES)),
            dma((8, PIECES)), dma((8, PIECES)),
            dma((6,)), dma((6,)),
            dma, dma,
            dma((15,)), dma((16,)),
            dma((12,)), dma((12,)),
            dma((3,)), dma((3,)),
            dma((CHUNKS,)), dma((CHUNKS,)),
            dma((CHUNKS, 2, 3)), dma((CHUNKS, 2, 3)),
            dma((CHUNKS, 8)), dma((CHUNKS, 8)),
        ],
        compiler_params=pltpu.CompilerParams(
            collective_id=0, has_side_effects=True, vmem_limit_bytes=58 * 1024 * 1024
        ),
        name="block",
    )(tokens, gain, w_planes, short_taps, taps, skip, w_out)


def per_device(tokens, norm_gain, w_in, short_taps, medium_taps, skip_gain, w_out):
    return block_call(
        tokens,
        norm_gain.reshape(16, 1, WIDE),
        jnp.transpose(w_in, (1, 0, 2)),
        short_taps,
        jnp.transpose(medium_taps),
        skip_gain.reshape(1, CH),
        w_out,
    )


def solution(mesh):
    in_specs = (
        P("seq", "chan"),
        P(),
        P("seq", None, "chan"),
        P(None, None, "chan"),
        P(None, "chan"),
        P("chan"),
        P("chan", None),
    )
    out_specs = P("seq", "chan")
    return jax.shard_map(
        per_device, mesh=mesh, in_specs=in_specs, out_specs=out_specs, check_vma=False
    )
```
